32 devices in a mesh: lon: 8 (over z, y), lat: 4 (over x, core).
Axes of the slice: x: 2, y: 2, z: 4, core: 2. Of those that a mesh axis runs over, the one named last changes fastest.
Arguments:
- zonal_velocity: float32 [40, 64, 1024], P(None, 'lat', 'lon'), as said below
- northward_velocity: float32 [40, 64, 1024], P(None, 'lat', 'lon'), as said below
- level_count: int32 [64, 1024], P('lat', 'lon'), may hold values from 0 to 40, as said below
- surface_height: float32 [64, 1024], P('lat', 'lon'), may hold values from -4 to 4
- zonal_transport: float32 [64, 1024], P('lat', 'lon'), may hold values from -4 to 4
- northward_transport: float32 [64, 1024], P('lat', 'lon'), may hold values from -4 to 4
- thickness: float32 [40], replicated, may hold values from 0.015 to 0.06
Outputs:
- zonal_after: float32 [40, 64, 1024], P(None, 'lat', 'lon')
- northward_after: float32 [40, 64, 1024], P(None, 'lat', 'lon')
- surface_after: float32 [64, 1024], P('lat', 'lon')
- zonal_mean: float32 [64, 1024], P('lat', 'lon')
- northward_mean: float32 [64, 1024], P('lat', 'lon')
The draws below stay inside these ranges and needn't reach their ends.
Inputs may be any that keep to these rules, and one draw needn't show every extreme that they name: `level_count`: ocean cells have 4 to 40 levels and land cells 0; the first and the last latitude rows are land. `zonal_velocity`: zero at every level k (counted from 0) with k >= min(level_count of the cell, level_count of its eastern neighbour), longitude wrapping. `northward_velocity`: zero at every level k (counted from 0) with k >= min(level_count of the cell, level_count of its northern neighbour), latitude wrapping.
All inputs are finite; a program needn't handle non-finite values.
Results may differ from the reference program's by a relative error of at most 0.0003.
Values sent between devices are 32-bit elements; how exact they have to be, the bound alone decides.
A program may use at most 64 MiB of HBM per device.

```python
import math
import jax
import jax.numpy as jnp
from jax import lax

CLAT = 16
CLON = 128
NZ = 40
NSUB = 30
NLAT = 64
NLON = 1024


def level_field(base_key):
    key_depth, key_coast, key_tiles = jax.random.split(jax.random.fold_in(base_key, 7), 3)
    depth = jax.random.randint(key_depth, (NLAT, NLON), 4, NZ + 1)
    coast = jax.random.randint(key_coast, (NLAT, NLON), 0, 5) == 0
    tiles = jax.random.randint(key_tiles, (NLAT // CLAT, NLON // CLON), 0, 8) == 0
    tiles = jnp.repeat(jnp.repeat(tiles, CLAT, 0), CLON, 1)
    row_index = jnp.arange(NLAT)[:, None]
    edges = (row_index == 0) | (row_index == NLAT - 1)
    return jnp.where(coast | tiles | edges, 0, depth).astype(jnp.int32)


def velocity_field(base_key, shift_axis, noise_tag):
    counts = level_field(base_key)
    face_count = jnp.minimum(counts, jnp.roll(counts, -1, shift_axis))
    wet_mask = jnp.arange(NZ)[:, None, None] < face_count[None]
    noise_key = jax.random.fold_in(base_key, noise_tag)
    values = jax.random.normal(noise_key, (NZ, NLAT, NLON), jnp.float32)
    return jnp.where(wet_mask, values, 0.0).astype(jnp.float32)


def draw_level_count(key, part):
    return level_field(key)


def draw_zonal_velocity(key, part):
    return velocity_field(key, -1, 11)


def draw_northward_velocity(key, part):
    return velocity_field(key, -2, 13)


def shard_levels(key, shape, pieces, smallest, top_value):
    def one(axis_at, blocks):
        heights = jax.random.uniform(jax.random.fold_in(jax.random.fold_in(key, 6), axis_at), (blocks,), jnp.float32, smallest / len(pieces), top_value / len(pieces))
        return jnp.repeat(jnp.exp(heights), shape[axis_at] // blocks).reshape((-1,) + (1,) * (len(shape) - axis_at - 1))

    loudness = one(*pieces[0])
    for cut in pieces[1:]:
        loudness = loudness * one(*cut)
    return loudness


def normal_values(own_key, extent, deviation, most, shards=(), kind=jnp.bfloat16):
    entries = jax.random.normal(own_key, extent, jnp.float32) * deviation
    if len(shards) > 0:
        entries = shard_levels(own_key, extent, shards, -0.22, 0.18) * entries
    return jnp.clip(entries, min=-most, max=most).astype(kind)


def setup_inputs(seed: int = 0) -> dict:
    keys = jax.random.split(jax.random.key(seed), 8)
    zonal_velocity = draw_zonal_velocity(jax.random.fold_in(keys[7], 71), 0)
    northward_velocity = draw_northward_velocity(jax.random.fold_in(keys[7], 71), 0)
    level_count = draw_level_count(jax.random.fold_in(keys[7], 71), 0)
    surface_height = normal_values(keys[3], (NLAT, NLON), 0.5, 4.0, ((0, 4), (1, 8)), jnp.float32)
    zonal_transport = normal_values(keys[4], (NLAT, NLON), 0.5, 4.0, ((0, 4), (1, 8)), jnp.float32)
    northward_transport = normal_values(keys[5], (NLAT, NLON), 0.5, 4.0, ((0, 4), (1, 8)), jnp.float32)
    thickness = jnp.clip(jnp.exp(jax.random.uniform(keys[6], (NZ,), jnp.float32, math.log(0.015), math.log(0.06))), 0.015, 0.06)
    return {"zonal_velocity": zonal_velocity, "northward_velocity": northward_velocity, "level_count": level_count, "surface_height": surface_height, "zonal_transport": zonal_transport, "northward_transport": northward_transport, "thickness": thickness}


viscosity = 0.01
timestep = 0.35


def eastward(grid_field):
    return jnp.roll(grid_field, -1, -1)


def westward(grid_field):
    return jnp.roll(grid_field, 1, -1)


def northward(grid_field):
    return jnp.roll(grid_field, -1, -2)


def southward(grid_field):
    return jnp.roll(grid_field, 1, -2)


def laplace(grid_field):
    return eastward(grid_field) + westward(grid_field) + northward(grid_field) + southward(grid_field) - 4.0 * grid_field


def substep(height, flux_east, flux_north, depth_east, depth_north, force_east, force_north):
    spread = flux_east - jnp.roll(flux_east, 1, -1) + flux_north - jnp.roll(flux_north, 1, -2)
    height = height - timestep * spread
    flux_east = flux_east - timestep * depth_east * (jnp.roll(height, -1, -1) - height) + timestep * force_east
    flux_north = flux_north - timestep * depth_north * (jnp.roll(height, -1, -2) - height) + timestep * force_north
    return height, flux_east, flux_north


def reference(zonal_velocity, northward_velocity, level_count, surface_height, zonal_transport, northward_transport, thickness):
    face_east = jnp.minimum(level_count, eastward(level_count))
    face_north = jnp.minimum(level_count, northward(level_count))
    layers = jnp.arange(NZ, dtype=jnp.int32)

    def tendency(grid_field, face_count, level_index):
        wet_mask = (level_index < face_count).astype(jnp.float32)
        return -viscosity * wet_mask * laplace(wet_mask * laplace(grid_field)), wet_mask

    def level_sums(running, inputs):
        zonal_level, north_level, layer_depth, level_index = inputs
        tend_east, wet_east = tendency(zonal_level, face_east, level_index)
        tend_north, wet_north = tendency(north_level, face_north, level_index)
        depth_east, depth_north, force_east, force_north, column_east, column_north = running
        return (depth_east + layer_depth * wet_east,
                depth_north + layer_depth * wet_north,
                force_east + layer_depth * tend_east,
                force_north + layer_depth * tend_north,
                column_east + layer_depth * (zonal_level + tend_east),
                column_north + layer_depth * (north_level + tend_north)), None

    zeros = jnp.zeros(level_count.shape, jnp.float32)
    sums, unused = lax.scan(level_sums, (zeros, zeros, zeros, zeros, zeros, zeros),
                            (zonal_velocity, northward_velocity, thickness, layers))
    depth_east, depth_north, force_east, force_north, column_east, column_north = sums
    force_east = force_east / (NSUB * timestep)
    force_north = force_north / (NSUB * timestep)
    open_east = (face_east > 0).astype(jnp.float32)
    open_north = (face_north > 0).astype(jnp.float32)
    height = surface_height
    flux_east = open_east * zonal_transport
    flux_north = open_north * northward_transport
    total_east = zeros
    total_north = zeros
    for repeat in range(NSUB):
        height, flux_east, flux_north = substep(height, flux_east, flux_north, depth_east, depth_north, force_east, force_north)
        total_east = total_east + flux_east
        total_north = total_north + flux_north
    mean_east = total_east / NSUB
    mean_north = total_north / NSUB
    shift_east = (mean_east - column_east) / (depth_east + 1.0 - open_east)
    shift_north = (mean_north - column_north) / (depth_north + 1.0 - open_north)

    def level_after(inputs):
        zonal_level, north_level, level_index = inputs
        tend_east, wet_east = tendency(zonal_level, face_east, level_index)
        tend_north, wet_north = tendency(north_level, face_north, level_index)
        return (wet_east * ((zonal_level + tend_east) + shift_east),
                wet_north * ((north_level + tend_north) + shift_north))

    zonal_after, northward_after = lax.map(level_after, (zonal_velocity, northward_velocity, layers))
    return (zonal_after, northward_after, height, mean_east, mean_north)
```

```python
import functools

import jax
import jax.numpy as jnp
from jax import lax
from jax.experimental import pallas as pl
from jax.experimental.pallas import tpu as pltpu
from jax.sharding import PartitionSpec as P

NSUB = 30
VISCOSITY = 0.01
TIMESTEP = 0.35
LANES = 128
GROUP = 4
PER_TILE = LANES // GROUP
UNROLL = 8
HALO = 32
MESH = pl.DeviceIdType.MESH


def lane_of(x):
    return lax.broadcasted_iota(jnp.int32, x.shape, 1)


def sub_of(x):
    return lax.broadcasted_iota(jnp.int32, x.shape, 0)


def lanes(x, shift):
    return pltpu.roll(x, shift % LANES, 1) if shift % LANES else x


def up(x):
    return pltpu.roll(x, x.shape[0] - 1, 0)


def down(x):
    return pltpu.roll(x, 1, 0)


def segments(layers):
    found, q = [], 0
    for field in range(2):
        k = 0
        while k < layers:
            n = min(layers - k, PER_TILE - q % PER_TILE)
            found.append((field, k, n, q // PER_TILE, q % PER_TILE))
            k, q = k + n, q + n
    return found


def kernel(
    nlon, nlat, tiles, centre,
    thick_hbm, ve_hbm, vn_hbm, cnt_hbm, height_hbm, te_hbm, tn_hbm,
    oe, on, small,
    thick, ve, vn, cnt, loads,
    rows_e, rows_n, packed, from_east, from_west, corner, corner_count, inject,
    count_north, count_south, count_east, count_west,
    state, side_out, side_in, force, force_out, force_in, plan,
    send, recv,
):
    layers, r, _ = ve.shape
    span = tiles * r
    nv = span // 8
    lon, lat = lax.axis_index("lon"), lax.axis_index("lat")
    offsets = [o for o in range(centre - tiles + 1, centre + 1) if o != 0]
    own = pl.ds(centre * r, r)

    def device(dx, dy):
        return {"lon": lax.rem(lon + nlon + dx, nlon), "lat": lax.rem(lat + nlat + dy, nlat)}

    partners = [(1, 0), (-1, 0)] + [(0, o) for o in offsets]
    partners += [(dx, o) for dx in (1, -1) for o in offsets]
    barrier = pltpu.get_barrier_semaphore()
    for dx, dy in partners:
        pl.semaphore_signal(barrier, inc=1, device_id=device(dx, dy), device_id_type=MESH)

    fetched = []
    for i, (far, near) in enumerate((
        (ve_hbm, ve), (vn_hbm, vn), (cnt_hbm, cnt), (height_hbm, state.at[1, own]), (te_hbm, state.at[2, own]),
        (tn_hbm, state.at[3, own]), (thick_hbm, thick),
    )):
        fetched.append(pltpu.make_async_copy(far, near, loads.at[i]))
        fetched[-1].start()

    used = [0]
    started = []

    def push(src, dst, dx, dy):
        i = used[0]
        used[0] += 1
        c = pltpu.make_async_remote_copy(
            src_ref=src, dst_ref=dst, send_sem=send.at[i], recv_sem=recv.at[i],
            device_id=device(dx, dy), device_id_type=MESH)
        c.start()
        started.append(c)
        return c

    for c in fetched:
        c.wait()

    ntiles = packed.shape[0]
    for t in range(ntiles):
        acc = jnp.zeros((r, LANES), jnp.float32)
        for field, k0, n, tile, m0 in segments(layers):
            if tile != t:
                continue
            v = (ve, vn)[field]

            def put(i, acc, v=v, k0=k0, m0=m0):
                m = m0 + i
                x = pltpu.roll(v[k0 + i], GROUP * m + 2 - LANES * ((GROUP * m + 2) // LANES), 1)
                return jnp.where(lane_of(x) // GROUP == m, x, acc)

            acc = lax.fori_loop(0, n, put, acc, unroll=4)
        packed[t] = acc
    pl.semaphore_wait(barrier, len(partners))

    lon_c = [push(cnt, count_west, 1, 0), push(cnt, count_east, -1, 0)]
    diag_c, diag_v, lat_v = [], [], []
    diag = [(-1, -1, 0), (-1, 1, 1), (1, -1, 2), (1, 1, 3)]
    low8, high8 = pl.ds(0, 8), pl.ds(r - 8, 8)
    for dx, dy, slot in diag:
        diag_c.append(push(cnt.at[low8 if dy < 0 else high8], corner_count.at[slot], dx, dy))
    lat_c = [push(cnt.at[low8], count_north, 0, -1), push(cnt.at[high8], count_south, 0, 1)]
    for dx, dy, slot in diag:
        diag_v.append(push(packed.at[:, low8 if dy < 0 else high8], corner.at[slot], dx, dy))
    lon_v = [push(packed, from_west, 1, 0), push(packed, from_east, -1, 0)]
    for v, buf in ((ve, rows_e), (vn, rows_n)):
        lat_v.append(push(v.at[:, pl.ds(0, 2)], buf.at[:, pl.ds(0, 2)], 0, -1))
        lat_v.append(push(v.at[:, pl.ds(r - 2, 2)], buf.at[:, pl.ds(6, 2)], 0, 1))

    zero = jnp.zeros((r, LANES), jnp.float32)
    cnt_own = cnt[...]

    def deepen(k, d):
        return jnp.where(k < cnt_own, d + thick[k], d)

    depth = lax.fori_loop(0, layers, deepen, zero, unroll=8)
    state[0, own] = depth
    four = [depth] + [state[f, own] for f in range(1, 4)]
    slot16 = lane_of(depth)
    west_side, east_side = four[0], lanes(four[0], HALO)
    for f in range(1, 4):
        here = slot16 // HALO == f
        west_side = jnp.where(here, lanes(four[f], HALO * f), west_side)
        east_side = jnp.where(here, lanes(four[f], HALO * f + HALO), east_side)
    side_out[0] = west_side
    side_out[1] = east_side

    def rows(o):
        return pl.ds((centre - o) * r, r)

    exchange_s = []
    for o in [0] + offsets:
        exchange_s.append(push(side_out.at[1], side_in.at[1, rows(o)], 1, o))
        exchange_s.append(push(side_out.at[0], side_in.at[0, rows(o)], -1, o))
    for o in offsets:
        exchange_s.append(push(state.at[:, own], state.at[:, rows(o)], 0, o))

    for c in lon_c + diag_c + lat_c:
        c.wait_recv()

    low = lax.broadcasted_iota(jnp.int32, (8, LANES), 0) < 4

    def ring(x, north, south):
        return jnp.concatenate([x, jnp.where(low, north, south)], 0)

    c24 = ring(cnt_own, count_north[...], count_south[...])
    ce = ring(count_east[...], corner_count[0], corner_count[1])
    cw = ring(count_west[...], corner_count[2], corner_count[3])
    lane = lane_of(c24)
    face_e = jnp.minimum(c24, jnp.where(lane == LANES - 1, lanes(ce, -1), lanes(c24, -1)))
    face_n = jnp.minimum(c24, up(c24))

    def spread(x):
        x = jnp.where(lane < 2, x, 0)
        step = GROUP
        while step < LANES:
            x = x + lanes(x, step)
            step *= 2
        return x

    inner = spread(jnp.where(lane == 0, ce, lanes(cw, 2)))
    outer = spread(jnp.where(lane == 0, lanes(ce, -1), lanes(c24, 1)))
    edge_e = jnp.minimum(inner, outer)[:r]
    edge_n = jnp.minimum(inner, up(inner))[:r]
    place = slot16 % GROUP
    for c in lon_v + diag_v:
        c.wait_recv()
    for t in range(ntiles):
        fe = ring(from_east[t], corner[0, t], corner[1, t])
        fw = ring(from_west[t], corner[2, t], corner[3, t])
        g = jnp.where(lane % GROUP == 0, lanes(fe, -2), fw)
        across = jnp.where(place == 0, lanes(fe[:r], -3), lanes(fw[:r], 1)) + lanes(packed[t], -1)
        q = t * PER_TILE + slot16 // GROUP
        k = jnp.where(q < layers, q, q - layers)
        wet = k < jnp.where(q < layers, edge_e, edge_n)
        e = jnp.where(wet, across + up(g)[:r] + down(g)[:r] - 4.0 * g[:r], 0.0)
        inject[t, 0:r] = jnp.where(place < 2, g[:r], lanes(e, 2))
        inject[t, r:r + 8] = g[r:]

    first, last = lane == 0, lane == LANES - 1
    first16, last16 = first[:r], last[:r]
    for c in lat_v:
        c.wait_recv()
    sums = []
    for field, (v, buf, face, out) in enumerate(((ve, rows_e, face_e, oe), (vn, rows_n, face_n, on))):

        def level(k, carry, field=field, v=v, buf=buf, face=face, out=out):
            total, column = carry
            q = field * layers + k
            t = q // PER_TILE
            m = q - t * PER_TILE
            own = v[k]
            x = jnp.concatenate([own, buf[k]], 0)
            j = inject[t]
            turn = LANES - 1 - GROUP * m
            turn = jnp.where(turn < 0, turn + LANES, turn)
            rim = pltpu.roll(j, turn, 1)
            rim2 = pltpu.roll(j[:r], jnp.where(turn < 2, turn + LANES - 2, turn - 2), 1)
            wet = k < face
            l1 = (jnp.where(last, rim, lanes(x, -1)) + jnp.where(first, rim, lanes(x, 1))
                  + up(x) + down(x) - 4.0 * x)
            l1 = jnp.where(wet, l1, 0.0)
            mid = l1[:r]
            l2 = (jnp.where(last16, rim2, lanes(mid, -1)) + jnp.where(first16, rim2, lanes(mid, 1))
                  + up(l1)[:r] + down(l1)[:r] - 4.0 * mid)
            tend = jnp.where(wet[:r], -VISCOSITY * l2, 0.0)
            after = own + tend
            out[k] = after
            return total + thick[k] * tend, column + thick[k] * after

        sums.append(lax.fori_loop(0, layers, level, (zero, zero), unroll=UNROLL))
    (sum_e, column_e), (sum_n, column_n) = sums
    force_tail(nlon, tiles, centre, r, offsets, push, rows, exchange_s, started, sum_e, sum_n, column_e, column_n,
               face_e[:r].astype(jnp.float32), face_n[:r].astype(jnp.float32),
               state, side_in, force, force_out, force_in, plan, small)


def force_tail(nlon, tiles, centre, r, offsets, push, rows, exchange_s, started, sum_e, sum_n, column_e, column_n,
               face_e, face_n, state, side_in, force, force_out, force_in, plan, small):
    span = tiles * r
    nv = span // 8
    own = pl.ds(centre * r, r)
    half = r // 2
    middle = LANES // 2
    sum_e, sum_n = sum_e * (TIMESTEP / NSUB), sum_n * (TIMESTEP / NSUB)
    force[0, own] = sum_e
    force[1, own] = sum_n
    lane = lane_of(sum_e)
    west_side = jnp.where(lane < HALO, sum_e, lanes(sum_n, HALO))
    east_side = jnp.where(lane < HALO, lanes(sum_e, HALO), lanes(sum_n, 2 * HALO))
    near = lane[:half] < middle
    force_out[0] = jnp.where(near, west_side[:half], lanes(west_side[half:], middle))
    force_out[1] = jnp.where(near, east_side[:half], lanes(east_side[half:], middle))
    exchange_f = []
    for o in [0] + offsets:
        part = pl.ds((centre - o) * half, half)
        exchange_f.append(push(force_out.at[1], force_in.at[1, part], 1, o))
        exchange_f.append(push(force_out.at[0], force_in.at[0, part], -1, o))
    for o in offsets:
        exchange_f.append(push(force.at[:, own], force.at[:, rows(o)], 0, o))

    for c in exchange_s:
        c.wait_recv()

    wide = lax.broadcasted_iota(jnp.int32, (span, LANES), 1)
    at_west, at_east = wide < HALO, wide >= LANES - HALO

    def blocks(mine, east, west, f):
        a = jnp.where(at_west, lanes(west, -HALO * f), lanes(mine, HALO))
        b = jnp.where(at_east, lanes(east, -HALO - HALO * f), lanes(mine, -HALO))
        return a, b

    def gate(depth, flux):
        return jnp.where(depth > 0, TIMESTEP * flux, 0.0)

    def divergence(x, y):
        return (x - lanes(x, 1)) + (y - down(y))

    square = TIMESTEP * TIMESTEP
    east, west = side_in[0], side_in[1]
    fields = [blocks(state[f], east, west, f) for f in range(4)]
    for b in range(2):
        d, h, te, tn = [x[b] for x in fields]
        de, dn = jnp.minimum(d, lanes(d, -1)), jnp.minimum(d, up(d))
        ae, an = square * de, square * dn
        aw, as_ = lanes(ae, 1), down(an)
        z = divergence(gate(de, te), gate(dn, tn))
        for i, x in enumerate((h, z, ae, aw, an, as_, ae + aw + an + as_)):
            plan[b, i] = x
    depth_own = state[0, own]
    over = state[0, pl.ds(((centre + 1) % tiles) * r, 8)]
    sub = sub_of(depth_own)
    depth_n = jnp.minimum(depth_own, jnp.where(sub == r - 1, pltpu.roll(
        jnp.concatenate([over] * (r // 8), 0), r - 1, 0), up(depth_own)))
    depth_e = jnp.minimum(depth_own, jnp.where(lane == LANES - 1, lanes(side_in[0, own], -1), lanes(depth_own, -1)))
    start_e, start_n = gate(depth_e, state[2, own]), gate(depth_n, state[3, own])

    for c in exchange_f:
        c.wait_recv()

    def unfold(x):
        return jnp.concatenate(
            [y for t in range(tiles) for y in (x[t * half:t * half + half], lanes(x[t * half:t * half + half], middle))], 0)

    east, west = unfold(force_in[0]), unfold(force_in[1])
    fe, fn = [blocks(force[f], east, west, f) for f in range(2)]
    for b in range(2):
        plan[b, 7] = divergence(fe[b], fn[b])

    def dealt(b, i):
        return jnp.concatenate([plan[b, i, pl.ds(v, 8, stride=nv)] for v in range(nv)], 0)

    def next_row(x):
        return jnp.concatenate([x[8:], pltpu.roll(x[:8], 7, 0)], 0)

    def prior_row(x):
        return jnp.concatenate([pltpu.roll(x[span - 8:], 1, 0), x[:span - 8]], 0)

    fixed = [[dealt(b, i) for i in range(2, 8)] for b in range(2)]
    begin = [dealt(b, 0) for b in range(2)] + [dealt(b, 1) for b in range(2)]
    begin += [jnp.zeros((span, LANES), jnp.float32)] * 2

    def step(i, carry):
        weight = (NSUB - i).astype(jnp.float32)
        hs, zs, us = [], [], []
        for b in range(2):
            h, z, u = carry[b], carry[2 + b], carry[4 + b]
            ae, aw, an, as_, ac, d = fixed[b]
            h = h - z
            z = z + ((ac * h + d) - (ae * lanes(h, -1) + aw * lanes(h, 1)) - (an * next_row(h) + as_ * prior_row(h)))
            hs.append(h)
            zs.append(z)
            us.append(u + weight * h)
        return (*hs, *zs, *us)

    done = lax.fori_loop(0, NSUB, step, tuple(begin), unroll=SUB_UNROLL)
    for b in range(2):
        for i, x in ((0, done[b]), (1, done[4 + b])):
            for v in range(nv):
                plan[b, i, pl.ds(v, 8, stride=nv)] = x[8 * v:8 * v + 8]

    left = lane < middle
    over = pl.ds(((centre + 1) % tiles) * r, 8)

    def joined(i, place):
        a, b = plan[0, i, place], plan[1, i, place]
        return a, b

    a, b = joined(0, own)
    final = jnp.where(left, lanes(a, -HALO), lanes(b, HALO))
    a, b = joined(1, own)
    u = jnp.where(left, lanes(a, -HALO), lanes(b, HALO))
    u_east = jnp.where(left, lanes(a, -HALO - 1), lanes(b, HALO - 1))
    a, b = joined(1, over)
    row = jnp.where(left[:8], lanes(a, -HALO), lanes(b, HALO))
    row = pltpu.roll(jnp.concatenate([row] * (r // 8), 0), r - 1, 0)
    u_north = jnp.where(sub == r - 1, row, up(u))
    ramp = NSUB * (NSUB + 1) / 2
    total_e = NSUB * start_e - square * depth_e * (u_east - u) + ramp * sum_e
    total_n = NSUB * start_n - square * depth_n * (u_north - u) + ramp * sum_n
    mean_e = total_e / (NSUB * TIMESTEP)
    mean_n = total_n / (NSUB * TIMESTEP)
    one = jnp.ones((r, LANES), jnp.float32)
    small[0] = final
    small[1] = mean_e
    small[2] = mean_n
    small[3] = (mean_e - column_e) / (depth_e + jnp.where(depth_e > 0, 0.0, one))
    small[4] = (mean_n - column_n) / (depth_n + jnp.where(depth_n > 0, 0.0, one))
    small[5] = face_e
    small[6] = face_n
    for c in started:
        c.wait_send()


SUB_UNROLL = 5


def finish(after_e, after_n, small, oe, on, oh, ome, omn):
    oh[...] = small[0]
    ome[...] = small[1]
    omn[...] = small[2]
    face_e, face_n = small[5], small[6]
    shift_e, shift_n = small[3], small[4]

    def level(k, _):
        depth = k.astype(jnp.float32)
        oe[k] = jnp.where(depth < face_e, after_e[k] + shift_e, 0.0)
        on[k] = jnp.where(depth < face_n, after_n[k] + shift_n, 0.0)
        return 0

    lax.fori_loop(0, after_e.shape[0], level, 0, unroll=4)


def solution(mesh):
    nlon, nlat = mesh.shape["lon"], mesh.shape["lat"]

    def shards(ve, vn, cnt, height, te, tn, thick):
        layers, r, width = ve.shape
        reach = -(-NSUB // r)
        tiles = min(nlat, 2 * reach + 1)
        centre = tiles // 2
        span = tiles * r
        ntiles = -(-2 * layers // PER_TILE)
        f32, i32 = jnp.float32, jnp.int32
        tile = (r, width)
        vm = pltpu.VMEM
        vspec = pl.BlockSpec(memory_space=pltpu.VMEM)
        copies = 2 + 4 + 2 + 4 + 2 + 4 + 2 * (3 * tiles - 1)
        after_e, after_n, small = pl.pallas_call(
            functools.partial(kernel, nlon, nlat, tiles, centre),
            out_shape=(
                jax.ShapeDtypeStruct(ve.shape, f32),
                jax.ShapeDtypeStruct(ve.shape, f32),
                jax.ShapeDtypeStruct((7, *tile), f32),
            ),
            in_specs=[pl.BlockSpec(memory_space=pltpu.HBM)] * 7,
            out_specs=[vspec] * 3,
            scratch_shapes=[
                pltpu.SMEM((layers,), f32),
                vm(ve.shape, f32),
                vm(ve.shape, f32),
                vm(tile, i32),
                pltpu.SemaphoreType.DMA((7,)),
                vm((layers, 8, width), f32),
                vm((layers, 8, width), f32),
                vm((ntiles, *tile), f32),
                vm((ntiles, *tile), f32),
                vm((ntiles, *tile), f32),
                vm((4, ntiles, 8, width), f32),
                vm((4, 8, width), i32),
                vm((ntiles, r + 8, width), f32),
                vm((8, width), i32),
                vm((8, width), i32),
                vm(tile, i32),
                vm(tile, i32),
                vm((4, span, width), f32),
                vm((2, *tile), f32),
                vm((2, span, width), f32),
                vm((2, span, width), f32),
                vm((2, r // 2, width), f32),
                vm((2, span // 2, width), f32),
                vm((2, 8, span, width), f32),
                pltpu.SemaphoreType.DMA((copies,)),
                pltpu.SemaphoreType.DMA((copies,)),
            ],
            compiler_params=pltpu.CompilerParams(
                collective_id=0, has_side_effects=True, vmem_limit_bytes=16 << 20),
        )(*[pltpu.with_memory_space_constraint(x, pltpu.HBM) for x in (thick, ve, vn, cnt, height, te, tn)])
        out = jax.ShapeDtypeStruct(tile, f32)
        levels = jax.ShapeDtypeStruct(ve.shape, f32)
        return pl.pallas_call(
            finish,
            out_shape=(levels, levels, out, out, out),
            in_specs=[vspec] * 3,
            out_specs=[vspec] * 5,
            compiler_params=pltpu.CompilerParams(vmem_limit_bytes=16 << 20),
        )(after_e, after_n, small)

    level = P(None, "lat", "lon")
    flat = P("lat", "lon")
    return jax.shard_map(
        shards,
        mesh=mesh,
        in_specs=(level, level, flat, flat, flat, flat, P()),
        out_specs=(level, level, flat, flat, flat),
        check_vma=False,
    )
```

```python
import functools
import math

import jax
import jax.numpy as jnp
from jax import lax
from jax.experimental import pallas as pl
from jax.experimental.pallas import tpu as pltpu
from jax.sharding import PartitionSpec as P

NSUB = 30
VISCOSITY = 0.01
TIMESTEP = 0.35
LANES = 128
GROUP = 4
HALO = 32
MESH = pl.DeviceIdType.MESH
EDGE, ROW_E, ROW_N, STATE, FORCE = range(5)


def lane_of(x):
    return lax.broadcasted_iota(jnp.int32, x.shape, 1)


def sub_of(x):
    return lax.broadcasted_iota(jnp.int32, x.shape, 0)


def lanes(x, shift):
    return pltpu.roll(x, shift % LANES, 1) if shift % LANES else x


def up(x):
    return pltpu.roll(x, x.shape[0] - 1, 0)


def down(x):
    return pltpu.roll(x, 1, 0)


def slots(group):
    return group // 4, LANES // 2 * (group % 2) + 2 * (group // 2 % 2)


def merge(parts, lane):
    bit = GROUP
    while len(parts) > 1:
        odd = lane // bit % 2 == 1
        parts = [jnp.where(odd, parts[i + 1], parts[i]) if i + 1 < len(parts) else parts[i] for i in range(0, len(parts), 2)]
        bit *= 2
    return parts[0]


def kernel(
    nlon, nlat, tiles, centre,
    thick_hbm, ve_hbm, vn_hbm, cnt_hbm, height_hbm, te_hbm, tn_hbm,
    oe, on, small,
    thick, ve, vn, cnt, loads,
    rows_e, rows_n, edges, from_east, from_west, corner_out, corner_in, rim, rim2, faces, keep, weights, counts,
    count_north, count_south,
    state, side_out, side_in, force, force_out, force_in, plan,
    send, recv,
):
    layers, r, _ = ve.shape
    groups = layers // 8
    lon, lat = lax.axis_index("lon"), lax.axis_index("lat")
    offsets = [o for o in range(centre - tiles + 1, centre + 1) if o != 0]
    own = pl.ds(centre * r, r)

    def device(dx, dy):
        return {"lon": lax.rem(lon + nlon + dx, nlon), "lat": lax.rem(lat + nlat + dy, nlat)}

    partners = [(1, 0), (-1, 0)] + [(0, o) for o in offsets]
    partners += [(dx, o) for dx in (1, -1) for o in offsets]
    barrier = pltpu.get_barrier_semaphore()
    for dx, dy in partners:
        pl.semaphore_signal(barrier, inc=1, device_id=device(dx, dy), device_id_type=MESH)

    fetched = []
    for i, far, near in (
        (0, ve_hbm, ve), (1, vn_hbm, vn), (2, cnt_hbm, cnt), (3, thick_hbm, thick),
        (4, height_hbm, state.at[1, own]), (4, te_hbm, state.at[2, own]), (4, tn_hbm, state.at[3, own]),
    ):
        fetched.append(pltpu.make_async_copy(far, near, loads.at[i]))
        fetched[-1].start()

    blank = plan.reshape(plan.shape[0] * plan.shape[1] * plan.shape[2], LANES)
    arriving = [0] * recv.shape[0]

    def push(kind, src, dst, dx, dy):
        pltpu.make_async_remote_copy(
            src_ref=src, dst_ref=dst, send_sem=send, recv_sem=recv.at[kind],
            device_id=device(dx, dy), device_id_type=MESH).start()
        arriving[kind] += math.prod(dst.shape) // LANES

    def settle(rows, sem):
        part = blank.at[pl.ds(0, rows)]
        pltpu.make_async_copy(part, part, sem).wait()

    def arrived(kind):
        settle(arriving[kind], recv.at[kind])

    low8, high8 = pl.ds(0, 8), pl.ds(r - 8, 8)
    pl.semaphore_wait(barrier, len(partners))
    push(EDGE, cnt_hbm.at[low8], count_north, 0, -1)
    push(EDGE, cnt_hbm.at[high8], count_south, 0, 1)
    for kind, v, buf in ((ROW_E, ve_hbm, rows_e), (ROW_N, vn_hbm, rows_n)):
        push(kind, v.at[:, pl.ds(0, 2)], buf.at[:, pl.ds(0, 2)], 0, -1)
        push(kind, v.at[:, pl.ds(r - 2, 2)], buf.at[:, pl.ds(6, 2)], 0, 1)

    for c in fetched[:4]:
        c.wait()

    vrows = [v.reshape(layers * r, LANES) for v in (ve, vn)]
    frows = [v.reshape(layers * 8, LANES) for v in (rows_e, rows_n)]
    orows = [v.reshape(layers * r, LANES) for v in (oe, on)]
    lane = lax.broadcasted_iota(jnp.int32, (8, LANES), 1)
    sub = lax.broadcasted_iota(jnp.int32, (8, LANES), 0)
    row_of = lane % (LANES // 2) // GROUP
    even, front = lane % 2 == 0, lane % GROUP < 2
    first, last = lane == 0, lane == LANES - 1

    cnt_own = cnt[...]
    counts[8:8 + r] = cnt_own.astype(jnp.float32)

    def spread_row(j):
        return jnp.broadcast_to(counts[8 + j:9 + j], (8, LANES))

    def column(g, j):
        if g == 2 * groups:
            return spread_row(j)
        return vrows[g // groups][pl.ds(8 * (g % groups) * r + j, 8, stride=r)]

    packs = []
    for t in range(groups + 1):
        parts = []
        for g in (2 * t, 2 * t + 1):
            if g <= 2 * groups:
                parts += [lanes(column(g, j), GROUP * len(parts) + GROUP * j + 2) for j in range(r)]
        packs.append(merge(parts, lane))
    ntiles = (groups + 2) // 2
    for u in range(ntiles):
        near, far = packs[2 * u], packs[min(2 * u + 1, groups)]
        edges[0, u] = jnp.where(front, lanes(near, -2), far)
        edges[1, u] = jnp.where(front, near, lanes(far, 2))
    diag = [(-1, -1, 0), (-1, 1, 1), (1, -1, 2), (1, 1, 3)]
    for dx, dy, slot in diag:
        j = 0 if dy < 0 else r - 1
        acc = lanes(edges[(dx + 1) // 2, 0], -GROUP * j)
        for u in range(1, ntiles):
            acc = jnp.where(row_of == u, lanes(edges[(dx + 1) // 2, u], GROUP * (u - j)), acc)
        corner_out[slot] = acc
    push(EDGE, edges.at[1], from_west, 1, 0)
    push(EDGE, edges.at[0], from_east, -1, 0)
    for dx, dy, slot in diag:
        push(EDGE, corner_out.at[slot], corner_in.at[slot], dx, dy)

    zero = jnp.zeros((r, LANES), jnp.float32)

    def deepen(k, d):
        return jnp.where(k < cnt_own, d + thick[k], d)

    depth = lax.fori_loop(0, layers, deepen, zero, unroll=8)
    state[0, own] = depth
    pltpu.make_async_copy(state.at[pl.ds(1, 3), own], state.at[pl.ds(1, 3), own], loads.at[4]).wait()
    four = [depth] + [state[f, own] for f in range(1, 4)]
    slot16 = lane_of(depth)
    west_side, east_side = four[0], lanes(four[0], HALO)
    for f in range(1, 4):
        here = slot16 // HALO == f
        west_side = jnp.where(here, lanes(four[f], HALO * f), west_side)
        east_side = jnp.where(here, lanes(four[f], HALO * f + HALO), east_side)
    side_out[0] = west_side
    side_out[1] = east_side

    def rows(o):
        return pl.ds((centre - o) * r, r)

    for o in [0] + offsets:
        push(STATE, side_out.at[1], side_in.at[1, rows(o)], 1, o)
        push(STATE, side_out.at[0], side_in.at[0, rows(o)], -1, o)
    for o in offsets:
        push(STATE, state.at[:, own], state.at[:, rows(o)], 0, o)

    def columns(k, carry):
        a, b = carry
        return a + thick[k] * ve[k], b + thick[k] * vn[k]

    column_e, column_n = lax.fori_loop(0, layers, columns, (zero, zero), unroll=8)
    for g in range(groups):
        w = jnp.zeros((8, LANES), jnp.float32)
        for i in range(8):
            w = jnp.where(sub == i, thick[8 * g + i], w)
        weights[g] = w

    arrived(EDGE)
    counts[0:8] = count_south[...].astype(jnp.float32)
    counts[8 + r:16 + r] = count_north[...].astype(jnp.float32)
    north = jnp.where(even, corner_in[0], corner_in[2])
    south = jnp.where(even, corner_in[1], corner_in[3])
    inner, outer, norths, souths = [], [], [], []
    for u in range(ntiles):
        fe, fw = from_east[u], from_west[u]
        h = jnp.where(even, fe, fw)
        rim[1 + u] = h
        inner.append(h)
        norths.append(jnp.where(row_of == r - 1, lanes(north, GROUP * (r - 1 - u)), lanes(h, -GROUP)))
        souths.append(jnp.where(row_of == 0, lanes(south, -GROUP * u), lanes(h, GROUP)))
        outer.append((fe, fw))
    rim[0] = south
    rim[1 + ntiles] = north
    uc, lc = slots(2 * groups)
    here = (lane // 2 % 2 == lc // 2 % 2) & (lane // (LANES // 2) == lc // (LANES // 2))

    def everywhere(x):
        x = jnp.where(here, x, 0.0)
        x = x + lanes(x, 2 if lc // 2 % 2 == 0 else -2)
        return x + lanes(x, LANES // 2)

    beyond = jnp.where(even, lanes(outer[uc][0], -1), lanes(edges[0, uc], 1))
    edge_e = everywhere(jnp.minimum(inner[uc], beyond))
    edge_n = everywhere(jnp.minimum(inner[uc], norths[uc]))
    for u in range(ntiles):
        fe, fw = outer[u]
        across = jnp.where(even, lanes(fe + edges[1, u], -1), lanes(fw + edges[0, u], 1))
        g = 4 * u + lane // 2 % 2 * 2 + lane // (LANES // 2)
        k = (jnp.where(g < groups, g, g - groups) * 8 + sub).astype(jnp.float32)
        wet = k < jnp.where(g < groups, edge_e, edge_n)
        rim2[u] = jnp.where(wet, (across - 4.0 * inner[u]) + (norths[u] + souths[u]), 0.0)

    here_row = [spread_row(j) for j in range(-1, r + 2)]
    for j in range(-1, r + 1):
        if j < 0:
            side = lanes(south, LANES - 1 - lc - GROUP * uc)
        elif j == r:
            side = lanes(north, LANES - 1 - lc - GROUP * uc)
        else:
            side = lanes(inner[uc], LANES - 1 - lc - GROUP * j)
        c = here_row[j + 1]
        face_e = jnp.minimum(c, jnp.where(last, side, lanes(c, -1)))
        face_n = jnp.minimum(c, here_row[j + 2])
        faces[0, 1 + j] = face_e
        faces[1, 1 + j] = face_n
        if 0 <= j < r:
            small[5, j:j + 1] = face_e[:1]
            small[6, j:j + 1] = face_n[:1]

    level_of = sub.astype(jnp.float32)

    def turned(ref, base, g, j):
        group = g
        u = group // 4
        shift = LANES // 2 * (group % 2) + 2 * (group // 2 % 2)
        shift = 2 * LANES - 1 - shift - GROUP * j
        return pltpu.roll(ref[base + u], shift % LANES, 1)

    def cross(x, side, n, s):
        e = jnp.where(last, side, lanes(x, -1))
        w = jnp.where(first, side, lanes(x, 1))
        return (e + w) + (n + s) - 4.0 * x

    def tendency(f, g, j, x, low, mid, high, wet):
        l2 = cross(mid, turned(rim2, 0, f * groups + g, j), high, low)
        tend = jnp.where(wet, -VISCOSITY * l2, 0.0)
        orows[f][pl.ds(8 * r * g + j, 8, stride=r)] = x + tend
        return weights[g] * tend

    def wetness(f, g, j):
        return level_of + 8.0 * g.astype(jnp.float32) < faces[f, 1 + j]

    totals = [[None] * r, [None] * r]
    none = jnp.zeros((8, LANES), jnp.float32)
    for f in range(2):

        def inside(g, carry, f=f):
            x = [vrows[f][pl.ds(8 * r * g + j, 8, stride=r)] for j in range(r)]
            wet = {j: wetness(f, g, j) for j in range(1, r - 1)}
            l1 = {}
            for j in range(1, r - 1):
                l1[j] = jnp.where(wet[j], cross(x[j], turned(rim, 1, f * groups + g, j), x[j + 1], x[j - 1]), 0.0)
            for i, j in enumerate((1, 2, r - 3, r - 2)):
                keep[f, g, i] = l1[j]
            return tuple(
                carry[j - 2] + tendency(f, g, j, x[j], l1[j - 1], l1[j], l1[j + 1], wet[j]) for j in range(2, r - 2))

        totals[f][2:r - 2] = lax.fori_loop(0, groups, inside, (none,) * (r - 4), unroll=INNER)

    arrived(ROW_E)
    arrived(ROW_N)
    for f in range(2):

        def border(g, carry, f=f):
            x = {j: vrows[f][pl.ds(8 * r * g + j, 8, stride=r)] for j in (0, 1, r - 2, r - 1)}
            for j, at in ((-2, 6), (-1, 7), (r, 0), (r + 1, 1)):
                x[j] = frows[f][pl.ds(64 * g + at, 8, stride=8)]
            wet = {j: wetness(f, g, j) for j in (-1, 0, 1, r - 2, r - 1, r)}
            l1 = {j: keep[f, g, i] for i, j in enumerate((1, 2, r - 3, r - 2))}
            for j in (-1, 0, r - 1, r):
                if j < 0 or j == r:
                    group = f * groups + g
                    shift = LANES // 2 * (group % 2) + 2 * (group // 2 % 2) + GROUP * (group // 4)
                    side = pltpu.roll(rim[0 if j < 0 else 1 + ntiles], (2 * LANES - 1 - shift) % LANES, 1)
                else:
                    side = turned(rim, 1, f * groups + g, j)
                l1[j] = jnp.where(wet[j], cross(x[j], side, x[j + 1], x[j - 1]), 0.0)
            return tuple(
                carry[i] + tendency(f, g, j, x[j], l1[j - 1], l1[j], l1[j + 1], wet[j])
                for i, j in enumerate((0, 1, r - 2, r - 1)))

        found = lax.fori_loop(0, groups, border, (none,) * 4, unroll=INNER)
        for i, j in enumerate((0, 1, r - 2, r - 1)):
            totals[f][j] = found[i]
    sub16 = sub_of(zero)
    sums = []
    for f in range(2):
        acc = zero
        for j in range(r):
            acc = jnp.where(sub16 == j, jnp.sum(totals[f][j], 0, keepdims=True), acc)
        sums.append(acc)
    sum_e, sum_n = sums
    force_tail(nlon, tiles, centre, r, offsets, push, arrived, rows, sum_e, sum_n, column_e + sum_e, column_n + sum_n,
               state, side_in, force, force_out, force_in, plan, small)
    settle(sum(arriving), send)


INNER = 5


def force_tail(nlon, tiles, centre, r, offsets, push, arrived, rows, sum_e, sum_n, column_e, column_n,
               state, side_in, force, force_out, force_in, plan, small):
    span = tiles * r
    nv = span // 8
    own = pl.ds(centre * r, r)
    half = r // 2
    middle = LANES // 2
    sum_e, sum_n = sum_e * (TIMESTEP / NSUB), sum_n * (TIMESTEP / NSUB)
    force[0, own] = sum_e
    force[1, own] = sum_n
    lane = lane_of(sum_e)
    west_side = jnp.where(lane < HALO, sum_e, lanes(sum_n, HALO))
    east_side = jnp.where(lane < HALO, lanes(sum_e, HALO), lanes(sum_n, 2 * HALO))
    near = lane[:half] < middle
    force_out[0] = jnp.where(near, west_side[:half], lanes(west_side[half:], middle))
    force_out[1] = jnp.where(near, east_side[:half], lanes(east_side[half:], middle))
    for o in [0] + offsets:
        part = pl.ds((centre - o) * half, half)
        push(FORCE, force_out.at[1], force_in.at[1, part], 1, o)
        push(FORCE, force_out.at[0], force_in.at[0, part], -1, o)
    for o in offsets:
        push(FORCE, force.at[:, own], force.at[:, rows(o)], 0, o)

    arrived(STATE)

    wide = lax.broadcasted_iota(jnp.int32, (span, LANES), 1)
    at_west, at_east = wide < HALO, wide >= LANES - HALO

    def blocks(mine, east, west, f):
        a = jnp.where(at_west, lanes(west, -HALO * f), lanes(mine, HALO))
        b = jnp.where(at_east, lanes(east, -HALO - HALO * f), lanes(mine, -HALO))
        return a, b

    def gate(depth, flux):
        return jnp.where(depth > 0, TIMESTEP * flux, 0.0)

    def divergence(x, y):
        return (x - lanes(x, 1)) + (y - down(y))

    def apply(m, x):
        mc, ae, aw, an, as_ = m
        return mc * x + (ae * lanes(x, -1) + aw * lanes(x, 1)) + (an * up(x) + as_ * down(x))

    square = TIMESTEP * TIMESTEP
    east, west = side_in[0], side_in[1]
    fields = [blocks(state[f], east, west, f) for f in range(4)]
    maps, ones, guess = [], [], []
    for b in range(2):
        d, h, te, tn = [x[b] for x in fields]
        de, dn = jnp.minimum(d, lanes(d, -1)), jnp.minimum(d, up(d))
        ae, an = square * de, square * dn
        aw, as_ = lanes(ae, 1), down(an)
        mc = 2.0 - ((ae + aw) + (an + as_))
        maps.append((mc, ae, aw, an, as_))
        h1 = h - divergence(gate(de, te), gate(dn, tn))
        ones.append(h1)
        guess.append(apply(maps[b], h1) - h)
        for i, x in enumerate((
            mc * mc + ((ae * ae + aw * aw) + (an * an + as_ * as_)) - 2.0,
            ae * (mc + lanes(mc, -1)), aw * (mc + lanes(mc, 1)), an * (mc + up(mc)), as_ * (mc + down(mc)),
            ae * lanes(ae, -1), aw * lanes(aw, 1), an * up(an), as_ * down(as_),
            ae * lanes(an, -1) + an * up(ae), ae * lanes(as_, -1) + as_ * down(ae),
            aw * lanes(an, 1) + an * up(aw), aw * lanes(as_, 1) + as_ * down(aw),
            h,
        )):
            plan[b, i] = x
    depth_own = state[0, own]
    over = state[0, pl.ds(((centre + 1) % tiles) * r, 8)]
    sub = sub_of(depth_own)
    depth_n = jnp.minimum(depth_own, jnp.where(
        sub == r - 1, pltpu.roll(jnp.concatenate([over] * (r // 8), 0), r - 1, 0), up(depth_own)))
    depth_e = jnp.minimum(depth_own, jnp.where(lane == LANES - 1, lanes(side_in[0, own], -1), lanes(depth_own, -1)))
    start_e, start_n = gate(depth_e, state[2, own]), gate(depth_n, state[3, own])

    arrived(FORCE)

    def unfold(x):
        return jnp.concatenate(
            [y for t in range(tiles) for y in (x[t * half:t * half + half], lanes(x[t * half:t * half + half], middle))], 0)

    east, west = unfold(force_in[0]), unfold(force_in[1])
    fe, fn = [blocks(force[f], east, west, f) for f in range(2)]
    drift = [divergence(fe[b], fn[b]) for b in range(2)]
    for b in range(2):
        plan[b, 14] = guess[b] - drift[b]
        plan[b, 15] = apply(maps[b], drift[b]) + 2.0 * drift[b]

    def dealt(b, i):
        return jnp.concatenate([plan[b, i, pl.ds(v, 8, stride=nv)] for v in range(nv)], 0)

    def next_row(x):
        return jnp.concatenate([x[8:], pltpu.roll(x[:8], 7, 0)], 0)

    def prior_row(x):
        return jnp.concatenate([pltpu.roll(x[span - 8:], 1, 0), x[:span - 8]], 0)

    pairs = NSUB // 2
    odd = [0] * (pairs + 1)
    for k in reversed(range(pairs)):
        odd[k] = NSUB - 2 * k - odd[k + 1]
    fixed = [[dealt(b, i) for i in range(13)] for b in range(2)]
    push_by = [dealt(b, 15) for b in range(2)]
    before = [dealt(b, 13) for b in range(2)]
    now = [dealt(b, 14) for b in range(2)]
    all_sum = [(NSUB - 1.0) * x for x in now]
    odd_sum = [float(odd[1]) * x for x in now]
    for k in range(2, pairs + 1):
        for b in range(2):
            h = now[b]
            c, e, w, n, s, ee, ww, nn, ss, en, es, wn, ws = fixed[b]
            he, hw, hn, hs = lanes(h, -1), lanes(h, 1), next_row(h), prior_row(h)
            core = (c * h - (before[b] + push_by[b])) + ((n * hn + s * hs) + (nn * next_row(hn) + ss * prior_row(hs)))
            side = (e * he + (en * next_row(he) + es * prior_row(he))) + (w * hw + (wn * next_row(hw) + ws * prior_row(hw)))
            before[b], now[b] = h, core + (side + (ee * lanes(h, -2) + ww * lanes(h, 2)))
            if k < pairs:
                odd_sum[b] += float(odd[k]) * now[b]
            all_sum[b] += (NSUB + 1.0 - 2 * k) * now[b]
    for b in range(2):
        for i, x in ((0, now[b]), (1, all_sum[b]), (2, odd_sum[b])):
            for v in range(nv):
                plan[b, i, pl.ds(v, 8, stride=nv)] = x[8 * v:8 * v + 8]

    left = lane < middle
    at = 8 if tiles >= 3 else centre * r
    low, size = (centre * r - 8, r + 16) if tiles >= 3 else (0, span)
    ends, here, easts, norths = [], [], [], []
    for b in range(2):
        m = [x[low:low + size] for x in maps[b]]
        total = (plan[b, 1, pl.ds(low, size)] + (odd[0] * ones[b][low:low + size] - float(sum(odd[1:])) * drift[b][low:low + size])
                 + apply(m, plan[b, 2, pl.ds(low, size)]))
        ends.append(plan[b, 0, own])
        here.append(total[at:at + r])
        easts.append(lanes(total, -1)[at:at + r])
        norths.append(up(total)[at:at + r])

    def joined(x):
        return jnp.where(left, lanes(x[0], -HALO), lanes(x[1], HALO))

    u, u_east, u_north = joined(here), joined(easts), joined(norths)
    ramp = NSUB * (NSUB + 1) / 2
    total_e = NSUB * start_e - square * depth_e * (u_east - u) + ramp * sum_e
    total_n = NSUB * start_n - square * depth_n * (u_north - u) + ramp * sum_n
    mean_e = total_e / (NSUB * TIMESTEP)
    mean_n = total_n / (NSUB * TIMESTEP)
    one = jnp.ones((r, LANES), jnp.float32)
    small[0] = joined(ends)
    small[1] = mean_e
    small[2] = mean_n
    small[3] = (mean_e - column_e) / (depth_e + jnp.where(depth_e > 0, 0.0, one))
    small[4] = (mean_n - column_n) / (depth_n + jnp.where(depth_n > 0, 0.0, one))


def finish(after_e, after_n, small, oe, on, oh, ome, omn):
    oh[...] = small[0]
    ome[...] = small[1]
    omn[...] = small[2]
    face_e, face_n = small[5], small[6]
    shift_e, shift_n = small[3], small[4]

    def level(k, _):
        depth = k.astype(jnp.float32)
        oe[k] = jnp.where(depth < face_e, after_e[k] + shift_e, 0.0)
        on[k] = jnp.where(depth < face_n, after_n[k] + shift_n, 0.0)
        return 0

    lax.fori_loop(0, after_e.shape[0], level, 0, unroll=4)


def solution(mesh):
    nlon, nlat = mesh.shape["lon"], mesh.shape["lat"]

    def shards(ve, vn, cnt, height, te, tn, thick):
        layers, r, width = ve.shape
        reach = -(-NSUB // r)
        tiles = min(nlat, 2 * reach + 1)
        centre = tiles // 2
        span = tiles * r
        groups = layers // 8
        ntiles = (groups + 2) // 2
        f32, i32 = jnp.float32, jnp.int32
        tile = (r, width)
        vm = pltpu.VMEM
        vspec = pl.BlockSpec(memory_space=pltpu.VMEM)
        after_e, after_n, small = pl.pallas_call(
            functools.partial(kernel, nlon, nlat, tiles, centre),
            out_shape=(
                jax.ShapeDtypeStruct(ve.shape, f32),
                jax.ShapeDtypeStruct(ve.shape, f32),
                jax.ShapeDtypeStruct((7, *tile), f32),
            ),
            in_specs=[pl.BlockSpec(memory_space=pltpu.HBM)] * 7,
            out_specs=[vspec] * 3,
            scratch_shapes=[
                pltpu.SMEM((layers,), f32),
                vm(ve.shape, f32),
                vm(ve.shape, f32),
                vm(tile, i32),
                pltpu.SemaphoreType.DMA((5,)),
                vm((layers, 8, width), f32),
                vm((layers, 8, width), f32),
                vm((2, ntiles, 8, width), f32),
                vm((ntiles, 8, width), f32),
                vm((ntiles, 8, width), f32),
                vm((4, 8, width), f32),
                vm((4, 8, width), f32),
                vm((ntiles + 2, 8, width), f32),
                vm((ntiles, 8, width), f32),
                vm((2, r + 2, 8, width), f32),
                vm((2, groups, 4, 8, width), f32),
                vm((groups, 8, width), f32),
                vm((r + 16, width), f32),
                vm((8, width), i32),
                vm((8, width), i32),
                vm((4, span, width), f32),
                vm((2, *tile), f32),
                vm((2, span, width), f32),
                vm((2, span, width), f32),
                vm((2, r // 2, width), f32),
                vm((2, span // 2, width), f32),
                vm((2, 17, span, width), f32),
                pltpu.SemaphoreType.DMA,
                pltpu.SemaphoreType.DMA((5,)),
            ],
            compiler_params=pltpu.CompilerParams(
                collective_id=0, has_side_effects=True, vmem_limit_bytes=16 << 20),
        )(*[pltpu.with_memory_space_constraint(x, pltpu.HBM) for x in (thick, ve, vn, cnt, height, te, tn)])
        out = jax.ShapeDtypeStruct(tile, f32)
        levels = jax.ShapeDtypeStruct(ve.shape, f32)
        return pl.pallas_call(
            finish,
            out_shape=(levels, levels, out, out, out),
            in_specs=[vspec] * 3,
            out_specs=[vspec] * 5,
            compiler_params=pltpu.CompilerParams(vmem_limit_bytes=16 << 20),
        )(after_e, after_n, small)

    level = P(None, "lat", "lon")
    flat = P("lat", "lon")
    return jax.shard_map(
        shards,
        mesh=mesh,
        in_specs=(level, level, flat, flat, flat, flat, P()),
        out_specs=(level, level, flat, flat, flat),
        check_vma=False,
    )
```

```python
import functools
import math

import jax
import jax.numpy as jnp
from jax import lax
from jax.experimental import pallas as pl
from jax.experimental.pallas import tpu as pltpu
from jax.sharding import PartitionSpec as P

NSUB = 30
VISCOSITY = 0.01
TIMESTEP = 0.35
LANES = 128
SLOT = 8
HALF = SLOT // 2
HALO = 32
MESH = pl.DeviceIdType.MESH
EDGE, ROW_E, ROW_N, STATE, FORCE = range(5)


def lane_of(x):
    return lax.broadcasted_iota(jnp.int32, x.shape, 1)


def sub_of(x):
    return lax.broadcasted_iota(jnp.int32, x.shape, 0)


def lanes(x, shift):
    return pltpu.roll(x, shift % LANES, 1) if shift % LANES else x


def up(x):
    return pltpu.roll(x, x.shape[0] - 1, 0)


def down(x):
    return pltpu.roll(x, 1, 0)


def merge(parts, lane):
    bit = SLOT
    while len(parts) > 1:
        odd = lane // bit % 2 == 1
        pairs = [(parts[i], parts[i + 1]) for i in range(0, len(parts), 2)]
        parts = [b if a is None else a if b is None else jnp.where(odd, b, a) for a, b in pairs]
        bit *= 2
    return parts[0]


def kernel(
    nlon, nlat, tiles, centre,
    thick_hbm, ve_hbm, vn_hbm, cnt_hbm, height_hbm, te_hbm, tn_hbm,
    oe, on, small,
    thick, ve, vn, cnt, loads,
    rows_e, rows_n, edges, from_east, from_west, corner_in, strip, faces, keep, weights, counts,
    count_north, count_south,
    state, side_out, side_in, force, force_out, force_in, plan,
    send, recv,
):
    layers, r, _ = ve.shape
    groups = layers // 8
    lon, lat = lax.axis_index("lon"), lax.axis_index("lat")
    offsets = [o for o in range(centre - tiles + 1, centre + 1) if o != 0]
    own = pl.ds(centre * r, r)

    def device(dx, dy):
        return {"lon": lax.rem(lon + nlon + dx, nlon), "lat": lax.rem(lat + nlat + dy, nlat)}

    partners = [(1, 0), (-1, 0)] + [(0, o) for o in offsets]
    partners += [(dx, o) for dx in (1, -1) for o in offsets]
    barrier = pltpu.get_barrier_semaphore()
    for dx, dy in partners:
        pl.semaphore_signal(barrier, inc=1, device_id=device(dx, dy), device_id_type=MESH)

    fetched = []
    for i, far, near in (
        (0, ve_hbm, ve), (1, vn_hbm, vn), (2, cnt_hbm, cnt), (3, thick_hbm, thick),
        (4, height_hbm, state.at[1, own]), (4, te_hbm, state.at[2, own]), (4, tn_hbm, state.at[3, own]),
    ):
        fetched.append(pltpu.make_async_copy(far, near, loads.at[i]))
        fetched[-1].start()

    blank = plan.reshape(plan.shape[0] * plan.shape[1] * plan.shape[2], LANES)
    arriving = [0] * recv.shape[0]

    def push(kind, src, dst, dx, dy):
        pltpu.make_async_remote_copy(
            src_ref=src, dst_ref=dst, send_sem=send, recv_sem=recv.at[kind],
            device_id=device(dx, dy), device_id_type=MESH).start()
        arriving[kind] += math.prod(dst.shape) // LANES

    def settle(rows, sem):
        part = blank.at[pl.ds(0, rows)]
        pltpu.make_async_copy(part, part, sem).wait()

    def arrived(kind):
        settle(arriving[kind], recv.at[kind])

    low8, high8 = pl.ds(0, 8), pl.ds(r - 8, 8)
    pl.semaphore_wait(barrier, len(partners))
    push(ROW_E, cnt_hbm.at[low8], count_north, 0, -1)
    push(ROW_E, cnt_hbm.at[high8], count_south, 0, 1)
    for kind, v, buf in ((ROW_E, ve_hbm, rows_e), (ROW_N, vn_hbm, rows_n)):
        push(kind, v.at[:, pl.ds(0, 2)], buf.at[:, pl.ds(0, 2)], 0, -1)
        push(kind, v.at[:, pl.ds(r - 2, 2)], buf.at[:, pl.ds(6, 2)], 0, 1)

    for c in fetched[:4]:
        c.wait()

    vrows = [v.reshape(layers * r, LANES) for v in (ve, vn)]
    frows = [v.reshape(layers * 8, LANES) for v in (rows_e, rows_n)]
    orows = [v.reshape(layers * r, LANES) for v in (oe, on)]
    lane = lax.broadcasted_iota(jnp.int32, (8, LANES), 1)
    sub = lax.broadcasted_iota(jnp.int32, (8, LANES), 0)
    slot = lane // SLOT
    start = lane % SLOT < HALF

    cnt_own = cnt[...]
    counts[8:8 + r] = cnt_own.astype(jnp.float32)

    def spread_row(j):
        return jnp.broadcast_to(counts[8 + j:9 + j], (8, LANES))

    def gathered(j, column):
        parts = [None] * (LANES // SLOT)
        for f in range(2):
            for g in range(groups):
                parts[LANES // SLOT // 2 * f + g] = column(f, g)
        parts[groups] = spread_row(j)
        parts = [None if x is None else lanes(x, SLOT * i + HALF) for i, x in enumerate(parts)]
        return merge(parts, lane)

    def own_column(j):
        return lambda f, g: vrows[f][pl.ds(8 * g * r + j, 8, stride=r)]

    for j in range(r):
        strip[2 + j] = gathered(j, own_column(j))
    for i in range(r // 2):
        a, b = strip[2 + 2 * i], strip[3 + 2 * i]
        edges[0, i] = jnp.where(start, lanes(b, -HALF), a)
        edges[1, i] = jnp.where(start, a, lanes(b, HALF))
    push(EDGE, edges.at[1], from_west, 1, 0)
    push(EDGE, edges.at[0], from_east, -1, 0)
    for dx, dy, at in ((-1, -1, 0), (-1, 1, 1), (1, -1, 2), (1, 1, 3)):
        push(EDGE, edges.at[(dx + 1) // 2, 0 if dy < 0 else r // 2 - 1], corner_in.at[at], dx, dy)

    zero = jnp.zeros((r, LANES), jnp.float32)

    def deepen(k, d):
        return jnp.where(k < cnt_own, d + thick[k], d)

    depth = lax.fori_loop(0, layers, deepen, zero, unroll=8)
    state[0, own] = depth
    pltpu.make_async_copy(state.at[pl.ds(1, 3), own], state.at[pl.ds(1, 3), own], loads.at[4]).wait()
    four = [depth] + [state[f, own] for f in range(1, 4)]
    slot16 = lane_of(depth)
    west_side, east_side = four[0], lanes(four[0], HALO)
    for f in range(1, 4):
        here = slot16 // HALO == f
        west_side = jnp.where(here, lanes(four[f], HALO * f), west_side)
        east_side = jnp.where(here, lanes(four[f], HALO * f + HALO), east_side)
    side_out[0] = west_side
    side_out[1] = east_side

    def rows(o):
        return pl.ds((centre - o) * r, r)

    for o in [0] + offsets:
        push(STATE, side_out.at[1], side_in.at[1, rows(o)], 1, o)
        push(STATE, side_out.at[0], side_in.at[0, rows(o)], -1, o)
    for o in offsets:
        push(STATE, state.at[:, own], state.at[:, rows(o)], 0, o)

    def columns(k, carry):
        a, b = carry
        return a + thick[k] * ve[k], b + thick[k] * vn[k]

    column_e, column_n = lax.fori_loop(0, layers, columns, (zero, zero), unroll=8)
    for g in range(groups):
        w = jnp.zeros((8, LANES), jnp.float32)
        for i in range(8):
            w = jnp.where(sub == i, thick[8 * g + i], w)
        weights[g] = w

    def face_rows(low, high):
        here = [spread_row(j) for j in range(low, high + 2)]
        for i, j in enumerate(range(low, high + 1)):
            c = here[i]
            faces[0, 1 + j] = jnp.minimum(c, lanes(c, -1))
            faces[1, 1 + j] = jnp.minimum(c, here[i + 1])

    face_rows(0, r - 2)
    level_of = sub.astype(jnp.float32)

    def cross(x, n, s):
        return (lanes(x, -1) + lanes(x, 1)) + (n + s) - 4.0 * x

    def tendency(f, g, j, x, low, mid, high, wet):
        l2 = cross(mid, high, low)
        tend = jnp.where(wet, -VISCOSITY * l2, 0.0)
        orows[f][pl.ds(8 * r * g + j, 8, stride=r)] = x + tend
        return weights[g] * tend

    def wetness(f, g, j):
        return level_of + 8.0 * g.astype(jnp.float32) < faces[f, 1 + j]

    totals = [[None] * r, [None] * r]
    none = jnp.zeros((8, LANES), jnp.float32)
    for f in range(2):

        def inside(g, carry, f=f):
            x = [vrows[f][pl.ds(8 * r * g + j, 8, stride=r)] for j in range(r)]
            wet = {j: wetness(f, g, j) for j in range(1, r - 1)}
            l1 = {}
            for j in range(1, r - 1):
                l1[j] = jnp.where(wet[j], cross(x[j], x[j + 1], x[j - 1]), 0.0)
            for i, j in enumerate((1, 2, r - 3, r - 2)):
                keep[f, g, i] = l1[j]
            return tuple(
                carry[j - 2] + tendency(f, g, j, x[j], l1[j - 1], l1[j], l1[j + 1], wet[j]) for j in range(2, r - 2))

        totals[f][2:r - 2] = lax.fori_loop(0, groups, inside, (none,) * (r - 4), unroll=INNER)

    for f in range(2):
        arrived((ROW_E, ROW_N)[f])
        if f == 0:
            counts[0:8] = count_south[...].astype(jnp.float32)
            counts[8 + r:16 + r] = count_north[...].astype(jnp.float32)
            face_rows(-1, -1)
            face_rows(r - 1, r)

        def border(g, carry, f=f):
            x = {j: vrows[f][pl.ds(8 * r * g + j, 8, stride=r)] for j in (0, 1, r - 2, r - 1)}
            for j, at in ((-2, 6), (-1, 7), (r, 0), (r + 1, 1)):
                x[j] = frows[f][pl.ds(64 * g + at, 8, stride=8)]
            wet = {j: wetness(f, g, j) for j in (-1, 0, 1, r - 2, r - 1, r)}
            l1 = {j: keep[f, g, i] for i, j in enumerate((1, 2, r - 3, r - 2))}
            for j in (-1, 0, r - 1, r):
                l1[j] = jnp.where(wet[j], cross(x[j], x[j + 1], x[j - 1]), 0.0)
            return tuple(
                carry[i] + tendency(f, g, j, x[j], l1[j - 1], l1[j], l1[j + 1], wet[j])
                for i, j in enumerate((0, 1, r - 2, r - 1)))

        found = lax.fori_loop(0, groups, border, (none,) * 4, unroll=INNER)
        for i, j in enumerate((0, 1, r - 2, r - 1)):
            totals[f][j] = found[i]
    sub16 = sub_of(zero)
    def stacked(rows_of):
        acc = zero
        for j in range(r):
            acc = jnp.where(sub16 == j, jnp.sum(rows_of[j], 0, keepdims=True), acc)
        return acc

    sum_e, sum_n = stacked(totals[0]), stacked(totals[1])
    half, middle = r // 2, LANES // 2
    scale = TIMESTEP / NSUB
    x, y = scale * sum_e, scale * sum_n
    west_side = jnp.where(slot16 < HALO, x, lanes(y, HALO))
    east_side = jnp.where(slot16 < HALO, lanes(x, HALO), lanes(y, 2 * HALO))
    near = slot16[:half] < middle
    force_out[0] = jnp.where(near, west_side[:half], lanes(west_side[half:], middle))
    force_out[1] = jnp.where(near, east_side[:half], lanes(east_side[half:], middle))
    for o in [0] + offsets:
        part = pl.ds((centre - o) * half, half)
        push(FORCE, force_out.at[1], force_in.at[1, part], 1, o)
        push(FORCE, force_out.at[0], force_in.at[0, part], -1, o)

    def far_column(at):
        return lambda f, g: frows[f][pl.ds(64 * g + at, 8, stride=8)]

    for j, at in ((-2, 6), (-1, 7), (r, 0), (r + 1, 1)):
        strip[2 + j] = gathered(j, far_column(at))
    arrived(EDGE)

    def unpacked(x, side, odd):
        return lanes(x, -HALF if side else HALF) if odd else x

    level_at = (SLOT * (slot % (LANES // SLOT // 2)) + sub).astype(jnp.float32)
    weight = jnp.zeros((8, LANES), jnp.float32)
    for g in range(groups):
        weight = jnp.where(slot % (LANES // SLOT // 2) == g, weights[g], weight)
    drops = []
    for side in range(2):
        source = from_west if side else from_east
        cells = []
        for j in range(-2, r + 2):
            if j < 0:
                far = unpacked(corner_in[2 * side + 1], side, j == -1)
            elif j >= r:
                far = unpacked(corner_in[2 * side], side, j == r + 1)
            else:
                far = unpacked(source[j // 2], side, j % 2)
            cells.append(jnp.where(start, far, strip[2 + j]) if side else jnp.where(start, strip[2 + j], far))
        wet, l1 = [], []
        for j in range(-1, r + 1):
            c = cells[2 + j]
            fe, fn = jnp.minimum(c, lanes(c, -1)), jnp.minimum(c, cells[3 + j])
            f = jnp.where(slot == 0, lanes(fe, -SLOT * groups), jnp.where(slot == SLOT, lanes(fn, SLOT * (SLOT - groups)), 0.0))
            for step in (SLOT, 2 * SLOT, 4 * SLOT):
                f = f + lanes(f, step)
            if side == 0 and 0 <= j < r:
                own_face = jnp.where(lane == LANES - 1, lanes(f, LANES - HALF), faces[0, 1 + j])
                small[5, j:j + 1] = own_face[:1]
                small[6, j:j + 1] = faces[1, 1 + j, 0:1]
            wet.append(level_at < f)
            l1.append(jnp.where(wet[-1], cross(c, cells[3 + j], cells[1 + j]), 0.0))
        drops.append([
            jnp.where(wet[1 + j], -VISCOSITY * cross(l1[1 + j], l1[2 + j], l1[j]), 0.0) for j in range(r)])
    found = []
    for side in range(2):
        x = stacked([weight * d for d in drops[side]])
        for step in (SLOT, 2 * SLOT, 4 * SLOT):
            x = x + lanes(x, -step)
        found.append(x)
    rim16 = (slot16 < 2) | (slot16 >= LANES - 2)
    at_start = slot16 < 2
    sum_e = jnp.where(rim16, jnp.where(at_start, lanes(found[1], -HALF), lanes(found[0], -HALF)), sum_e)
    sum_n = jnp.where(rim16, jnp.where(at_start, lanes(found[1], -HALF - middle), lanes(found[0], -HALF - middle)), sum_n)
    force[0, own] = scale * sum_e
    force[1, own] = scale * sum_n
    force[2, own] = scale * jnp.where(slot16 % SLOT < HALF, found[1], found[0])
    for o in offsets:
        push(FORCE, force.at[:, own], force.at[:, rows(o)], 0, o)
    rim = (lane < 2) | (lane >= LANES - 2)
    for j in range(r):
        ends = jnp.where(start, drops[0][j], drops[1][j])
        for f in range(2):
            for g in range(groups):
                at = pl.ds(8 * r * g + j, 8, stride=r)
                orows[f][at] = jnp.where(
                    rim, vrows[f][at] + lanes(ends, -SLOT * (SLOT * f + g) - HALF), orows[f][at])
    force_tail(tiles, centre, r, arrived, scale * sum_e, scale * sum_n, column_e + sum_e, column_n + sum_n,
               state, side_in, force, force_in, plan, small)
    settle(sum(arriving), send)


INNER = 5


def force_tail(tiles, centre, r, arrived, sum_e, sum_n, column_e, column_n, state, side_in, force, force_in, plan, small):
    span = tiles * r
    nv = span // 8
    own = pl.ds(centre * r, r)
    half = r // 2
    middle = LANES // 2
    lane = lane_of(sum_e)
    arrived(STATE)

    wide = lax.broadcasted_iota(jnp.int32, (span, LANES), 1)
    at_west, at_east = wide < HALO, wide >= LANES - HALO

    def blocks(mine, east, west, f):
        a = jnp.where(at_west, lanes(west, -HALO * f), lanes(mine, HALO))
        b = jnp.where(at_east, lanes(east, -HALO - HALO * f), lanes(mine, -HALO))
        return a, b

    def gate(depth, flux):
        return jnp.where(depth > 0, TIMESTEP * flux, 0.0)

    def divergence(x, y):
        return (x - lanes(x, 1)) + (y - down(y))

    def apply(m, x):
        mc, ae, aw, an, as_ = m
        return mc * x + (ae * lanes(x, -1) + aw * lanes(x, 1)) + (an * up(x) + as_ * down(x))

    square = TIMESTEP * TIMESTEP
    east, west = side_in[0], side_in[1]
    fields = [blocks(state[f], east, west, f) for f in range(4)]
    maps, ones, guess = [], [], []
    for b in range(2):
        d, h, te, tn = [x[b] for x in fields]
        de, dn = jnp.minimum(d, lanes(d, -1)), jnp.minimum(d, up(d))
        ae, an = square * de, square * dn
        aw, as_ = lanes(ae, 1), down(an)
        mc = 2.0 - ((ae + aw) + (an + as_))
        maps.append((mc, ae, aw, an, as_))
        h1 = h - divergence(gate(de, te), gate(dn, tn))
        ones.append(h1)
        guess.append(apply(maps[b], h1) - h)
        for i, x in enumerate((
            mc * mc + ((ae * ae + aw * aw) + (an * an + as_ * as_)) - 2.0,
            ae * (mc + lanes(mc, -1)), aw * (mc + lanes(mc, 1)), an * (mc + up(mc)), as_ * (mc + down(mc)),
            ae * lanes(ae, -1), aw * lanes(aw, 1), an * up(an), as_ * down(as_),
            ae * lanes(an, -1) + an * up(ae), ae * lanes(as_, -1) + as_ * down(ae),
            aw * lanes(an, 1) + an * up(aw), aw * lanes(as_, 1) + as_ * down(aw),
            h,
        )):
            plan[b, i] = x
    depth_own = state[0, own]
    over = state[0, pl.ds(((centre + 1) % tiles) * r, 8)]
    sub = sub_of(depth_own)
    depth_n = jnp.minimum(depth_own, jnp.where(
        sub == r - 1, pltpu.roll(jnp.concatenate([over] * (r // 8), 0), r - 1, 0), up(depth_own)))
    depth_e = jnp.minimum(depth_own, jnp.where(lane == LANES - 1, lanes(side_in[0, own], -1), lanes(depth_own, -1)))
    start_e, start_n = gate(depth_e, state[2, own]), gate(depth_n, state[3, own])

    arrived(FORCE)

    def unfold(x):
        return jnp.concatenate(
            [y for t in range(tiles) for y in (x[t * half:t * half + half], lanes(x[t * half:t * half + half], middle))], 0)

    east, west = unfold(force_in[0]), unfold(force_in[1])
    seam, rim_a, rim_b = force[2], at_west & (wide >= HALO - 2), at_east & (wide < LANES - HALO + 2)
    sides = []
    for f in range(2):
        a, b = blocks(force[f], east, west, f)
        a = jnp.where(rim_a, lanes(seam, HALO - HALF - middle * f), a)
        b = jnp.where(rim_b, lanes(seam, LANES - HALO - HALF - middle * f), b)
        sides.append((a, b))
    fe, fn = sides
    drift = [divergence(fe[b], fn[b]) for b in range(2)]
    for b in range(2):
        plan[b, 14] = guess[b] - drift[b]
        plan[b, 15] = apply(maps[b], drift[b]) + 2.0 * drift[b]

    def dealt(b, i):
        return jnp.concatenate([plan[b, i, pl.ds(v, 8, stride=nv)] for v in range(nv)], 0)

    def next_row(x):
        return jnp.concatenate([x[8:], pltpu.roll(x[:8], 7, 0)], 0)

    def prior_row(x):
        return jnp.concatenate([pltpu.roll(x[span - 8:], 1, 0), x[:span - 8]], 0)

    pairs = NSUB // 2
    odd = [0] * (pairs + 1)
    for k in reversed(range(pairs)):
        odd[k] = NSUB - 2 * k - odd[k + 1]
    fixed = [[dealt(b, i) for i in range(13)] for b in range(2)]
    push_by = [dealt(b, 15) for b in range(2)]
    before = [dealt(b, 13) for b in range(2)]
    now = [dealt(b, 14) for b in range(2)]
    all_sum = [(NSUB - 1.0) * x for x in now]
    odd_sum = [float(odd[1]) * x for x in now]
    for k in range(2, pairs + 1):
        for b in range(2):
            h = now[b]
            c, e, w, n, s, ee, ww, nn, ss, en, es, wn, ws = fixed[b]
            he, hw, hn, hs = lanes(h, -1), lanes(h, 1), next_row(h), prior_row(h)
            core = (c * h - (before[b] + push_by[b])) + ((n * hn + s * hs) + (nn * next_row(hn) + ss * prior_row(hs)))
            side = (e * he + (en * next_row(he) + es * prior_row(he))) + (w * hw + (wn * next_row(hw) + ws * prior_row(hw)))
            before[b], now[b] = h, core + (side + (ee * lanes(h, -2) + ww * lanes(h, 2)))
            if k < pairs:
                odd_sum[b] += float(odd[k]) * now[b]
            all_sum[b] += (NSUB + 1.0 - 2 * k) * now[b]
    for b in range(2):
        for i, x in ((0, now[b]), (1, all_sum[b]), (2, odd_sum[b])):
            for v in range(nv):
                plan[b, i, pl.ds(v, 8, stride=nv)] = x[8 * v:8 * v + 8]

    left = lane < middle
    at = 8 if tiles >= 3 else centre * r
    low, size = (centre * r - 8, r + 16) if tiles >= 3 else (0, span)
    ends, here, easts, norths = [], [], [], []
    for b in range(2):
        m = [x[low:low + size] for x in maps[b]]
        total = (plan[b, 1, pl.ds(low, size)] + (odd[0] * ones[b][low:low + size] - float(sum(odd[1:])) * drift[b][low:low + size])
                 + apply(m, plan[b, 2, pl.ds(low, size)]))
        ends.append(plan[b, 0, own])
        here.append(total[at:at + r])
        easts.append(lanes(total, -1)[at:at + r])
        norths.append(up(total)[at:at + r])

    def joined(x):
        return jnp.where(left, lanes(x[0], -HALO), lanes(x[1], HALO))

    u, u_east, u_north = joined(here), joined(easts), joined(norths)
    ramp = NSUB * (NSUB + 1) / 2
    total_e = NSUB * start_e - square * depth_e * (u_east - u) + ramp * sum_e
    total_n = NSUB * start_n - square * depth_n * (u_north - u) + ramp * sum_n
    mean_e = total_e / (NSUB * TIMESTEP)
    mean_n = total_n / (NSUB * TIMESTEP)
    one = jnp.ones((r, LANES), jnp.float32)
    small[0] = joined(ends)
    small[1] = mean_e
    small[2] = mean_n
    small[3] = (mean_e - column_e) / (depth_e + jnp.where(depth_e > 0, 0.0, one))
    small[4] = (mean_n - column_n) / (depth_n + jnp.where(depth_n > 0, 0.0, one))


def finish(after_e, after_n, small, oe, on, oh, ome, omn):
    oh[...] = small[0]
    ome[...] = small[1]
    omn[...] = small[2]
    face_e, face_n = small[5], small[6]
    shift_e, shift_n = small[3], small[4]

    def level(k, _):
        depth = k.astype(jnp.float32)
        oe[k] = jnp.where(depth < face_e, after_e[k] + shift_e, 0.0)
        on[k] = jnp.where(depth < face_n, after_n[k] + shift_n, 0.0)
        return 0

    lax.fori_loop(0, after_e.shape[0], level, 0, unroll=4)


def solution(mesh):
    nlon, nlat = mesh.shape["lon"], mesh.shape["lat"]

    def shards(ve, vn, cnt, height, te, tn, thick):
        layers, r, width = ve.shape
        reach = -(-NSUB // r)
        tiles = min(nlat, 2 * reach + 1)
        centre = tiles // 2
        span = tiles * r
        groups = layers // 8
        f32, i32 = jnp.float32, jnp.int32
        tile = (r, width)
        vm = pltpu.VMEM
        vspec = pl.BlockSpec(memory_space=pltpu.VMEM)
        after_e, after_n, small = pl.pallas_call(
            functools.partial(kernel, nlon, nlat, tiles, centre),
            out_shape=(
                jax.ShapeDtypeStruct(ve.shape, f32),
                jax.ShapeDtypeStruct(ve.shape, f32),
                jax.ShapeDtypeStruct((7, *tile), f32),
            ),
            in_specs=[pl.BlockSpec(memory_space=pltpu.HBM)] * 7,
            out_specs=[vspec] * 3,
            scratch_shapes=[
                pltpu.SMEM((layers,), f32),
                vm(ve.shape, f32),
                vm(ve.shape, f32),
                vm(tile, i32),
                pltpu.SemaphoreType.DMA((5,)),
                vm((layers, 8, width), f32),
                vm((layers, 8, width), f32),
                vm((2, r // 2, 8, width), f32),
                vm((r // 2, 8, width), f32),
                vm((r // 2, 8, width), f32),
                vm((4, 8, width), f32),
                vm((r + 4, 8, width), f32),
                vm((2, r + 2, 8, width), f32),
                vm((2, groups, 4, 8, width), f32),
                vm((groups, 8, width), f32),
                vm((r + 16, width), f32),
                vm((8, width), i32),
                vm((8, width), i32),
                vm((4, span, width), f32),
                vm((2, *tile), f32),
                vm((2, span, width), f32),
                vm((3, span, width), f32),
                vm((2, r // 2, width), f32),
                vm((2, span // 2, width), f32),
                vm((2, 17, span, width), f32),
                pltpu.SemaphoreType.DMA,
                pltpu.SemaphoreType.DMA((5,)),
            ],
            compiler_params=pltpu.CompilerParams(
                collective_id=0, has_side_effects=True, vmem_limit_bytes=16 << 20),
        )(*[pltpu.with_memory_space_constraint(x, pltpu.HBM) for x in (thick, ve, vn, cnt, height, te, tn)])
        out = jax.ShapeDtypeStruct(tile, f32)
        levels = jax.ShapeDtypeStruct(ve.shape, f32)
        return pl.pallas_call(
            finish,
            out_shape=(levels, levels, out, out, out),
            in_specs=[vspec] * 3,
            out_specs=[vspec] * 5,
            compiler_params=pltpu.CompilerParams(vmem_limit_bytes=16 << 20),
        )(after_e, after_n, small)

    level = P(None, "lat", "lon")
    flat = P("lat", "lon")
    return jax.shard_map(
        shards,
        mesh=mesh,
        in_specs=(level, level, flat, flat, flat, flat, P()),
        out_specs=(level, level, flat, flat, flat),
        check_vma=False,
    )
```

```python
import functools
import math

import jax
import jax.numpy as jnp
from jax import lax
from jax.experimental import pallas as pl
from jax.experimental.pallas import tpu as pltpu
from jax.sharding import PartitionSpec as P

NSUB = 30
VISCOSITY = 0.01
TIMESTEP = 0.35
LANES = 128
SLOT = 8
HALF = SLOT // 2
HALO = 32
MESH = pl.DeviceIdType.MESH
COUNT, EDGE, SOUTHWARD, NORTHWARD, STATE, FORCE = range(6)


def lane_of(x):
    return lax.broadcasted_iota(jnp.int32, x.shape, 1)


def sub_of(x):
    return lax.broadcasted_iota(jnp.int32, x.shape, 0)


def lanes(x, shift):
    return pltpu.roll(x, shift % LANES, 1) if shift % LANES else x


def up(x):
    return pltpu.roll(x, x.shape[0] - 1, 0)


def down(x):
    return pltpu.roll(x, 1, 0)


def merge(parts, lane):
    bit = SLOT
    while len(parts) > 1:
        odd = lane // bit % 2 == 1
        pairs = [(parts[i], parts[i + 1]) for i in range(0, len(parts), 2)]
        parts = [b if a is None else a if b is None else jnp.where(odd, b, a) for a, b in pairs]
        bit *= 2
    return parts[0]


def kernel(
    nlon, nlat, tiles, centre,
    thick_hbm, ve_hbm, vn_hbm, cnt_hbm, height_hbm, te_hbm, tn_hbm,
    oe, on, small,
    thick, ve, vn, cnt, loads,
    rows_e, rows_n, edges, from_east, from_west, corner_in, strip, faces, keep, weights, counts,
    count_north, count_south,
    state, side_out, side_in, force, force_out, force_in, seam, plan,
    send, recv,
):
    layers, r, _ = ve.shape
    groups = layers // 8
    lon, lat = lax.axis_index("lon"), lax.axis_index("lat")
    offsets = [o for o in range(centre - tiles + 1, centre + 1) if o != 0]
    own = pl.ds(centre * r, r)

    def device(dx, dy):
        return {"lon": lax.rem(lon + nlon + dx, nlon), "lat": lax.rem(lat + nlat + dy, nlat)}

    partners = [(1, 0), (-1, 0)] + [(0, o) for o in offsets]
    partners += [(dx, o) for dx in (1, -1) for o in offsets]
    barrier = pltpu.get_barrier_semaphore()
    for dx, dy in partners:
        pl.semaphore_signal(barrier, inc=1, device_id=device(dx, dy), device_id_type=MESH)

    fetched = []
    for i, far, near in (
        (0, ve_hbm, ve), (1, vn_hbm, vn), (2, cnt_hbm, cnt), (3, thick_hbm, thick),
        (4, height_hbm, state.at[1, own]), (4, te_hbm, state.at[2, own]), (4, tn_hbm, state.at[3, own]),
    ):
        fetched.append(pltpu.make_async_copy(far, near, loads.at[i]))
        fetched[-1].start()

    blank = plan.reshape(plan.shape[0] * plan.shape[1] * plan.shape[2], LANES)
    arriving = [0] * recv.shape[0]

    def sender(kind):
        return {SOUTHWARD: 1, NORTHWARD: 2}.get(kind, 0)

    def push(kind, src, dst, dx, dy):
        pltpu.make_async_remote_copy(
            src_ref=src, dst_ref=dst, send_sem=send.at[sender(kind)], recv_sem=recv.at[kind],
            device_id=device(dx, dy), device_id_type=MESH).start()
        arriving[kind] += math.prod(dst.shape) // LANES

    def settle(rows, sem):
        part = blank.at[pl.ds(0, rows)]
        pltpu.make_async_copy(part, part, sem).wait()

    def arrived(kind):
        settle(arriving[kind], recv.at[kind])

    low8, high8 = pl.ds(0, 8), pl.ds(r - 8, 8)
    pl.semaphore_wait(barrier, len(partners))
    @pl.when(lat > 0)
    def _():
        for v, buf in ((ve_hbm, rows_e), (vn_hbm, rows_n)):
            push(SOUTHWARD, v.at[:, pl.ds(0, 2)], buf.at[:, pl.ds(0, 2)], 0, -1)

    @pl.when(lat < nlat - 1)
    def _():
        for v, buf in ((ve_hbm, rows_e), (vn_hbm, rows_n)):
            push(NORTHWARD, v.at[:, pl.ds(r - 2, 2)], buf.at[:, pl.ds(6, 2)], 0, 1)

    push(COUNT, cnt_hbm.at[low8], count_north, 0, -1)
    push(COUNT, cnt_hbm.at[high8], count_south, 0, 1)

    for c in fetched[:4]:
        c.wait()

    vrows = [v.reshape(layers * r, LANES) for v in (ve, vn)]
    frows = [v.reshape(layers * 8, LANES) for v in (rows_e, rows_n)]
    orows = [v.reshape(layers * r, LANES) for v in (oe, on)]
    lane = lax.broadcasted_iota(jnp.int32, (8, LANES), 1)
    sub = lax.broadcasted_iota(jnp.int32, (8, LANES), 0)
    slot = lane // SLOT
    start = lane % SLOT < HALF

    cnt_own = cnt[...]
    counts[8:8 + r] = cnt_own.astype(jnp.float32)

    def spread_row(j):
        return jnp.broadcast_to(counts[8 + j:9 + j], (8, LANES))

    def gathered(j, column):
        parts = [None] * (LANES // SLOT)
        for f in range(2):
            for g in range(groups):
                parts[LANES // SLOT // 2 * f + g] = column(f, g)
        parts[groups] = spread_row(j)
        parts = [None if x is None else lanes(x, SLOT * i + HALF) for i, x in enumerate(parts)]
        return merge(parts, lane)

    def own_column(j):
        return lambda f, g: vrows[f][pl.ds(8 * g * r + j, 8, stride=r)]

    for j in range(r):
        strip[2 + j] = gathered(j, own_column(j))
    for i in range(r // 2):
        a, b = strip[2 + 2 * i], strip[3 + 2 * i]
        edges[0, i] = jnp.where(start, lanes(b, -HALF), a)
        edges[1, i] = jnp.where(start, a, lanes(b, HALF))
    push(EDGE, edges.at[1], from_west, 1, 0)
    push(EDGE, edges.at[0], from_east, -1, 0)
    for dx, dy, at in ((-1, -1, 0), (-1, 1, 1), (1, -1, 2), (1, 1, 3)):
        push(EDGE, edges.at[(dx + 1) // 2, 0 if dy < 0 else r // 2 - 1], corner_in.at[at], dx, dy)

    zero = jnp.zeros((r, LANES), jnp.float32)

    def deepen(k, d):
        return jnp.where(k < cnt_own, d + thick[k], d)

    depth = lax.fori_loop(0, layers, deepen, zero, unroll=8)
    state[0, own] = depth
    pltpu.make_async_copy(state.at[pl.ds(1, 3), own], state.at[pl.ds(1, 3), own], loads.at[4]).wait()
    four = [depth] + [state[f, own] for f in range(1, 4)]
    slot16 = lane_of(depth)
    west_side, east_side = four[0], lanes(four[0], HALO)
    for f in range(1, 4):
        here = slot16 // HALO == f
        west_side = jnp.where(here, lanes(four[f], HALO * f), west_side)
        east_side = jnp.where(here, lanes(four[f], HALO * f + HALO), east_side)
    side_out[0] = west_side
    side_out[1] = east_side

    def rows(o):
        return pl.ds((centre - o) * r, r)

    for o in [0] + offsets:
        push(STATE, side_out.at[1], side_in.at[1, rows(o)], 1, o)
        push(STATE, side_out.at[0], side_in.at[0, rows(o)], -1, o)
    for o in offsets:
        push(STATE, state.at[:, own], state.at[:, rows(o)], 0, o)

    def columns(k, carry):
        a, b = carry
        return a + thick[k] * ve[k], b + thick[k] * vn[k]

    column_e, column_n = lax.fori_loop(0, layers, columns, (zero, zero), unroll=8)
    for g in range(groups):
        w = jnp.zeros((8, LANES), jnp.float32)
        for i in range(8):
            w = jnp.where(sub == i, thick[8 * g + i], w)
        weights[g] = w

    def face_rows(low, high):
        here = [spread_row(j) for j in range(low, high + 2)]
        for i, j in enumerate(range(low, high + 1)):
            c = here[i]
            faces[0, 1 + j] = jnp.minimum(c, lanes(c, -1))
            faces[1, 1 + j] = jnp.minimum(c, here[i + 1])

    face_rows(0, r - 2)
    level_of = sub.astype(jnp.float32)

    def cross(x, n, s):
        return (lanes(x, -1) + lanes(x, 1)) + (n + s) - 4.0 * x

    def tendency(f, g, j, x, low, mid, high, wet):
        l2 = cross(mid, high, low)
        tend = jnp.where(wet, -VISCOSITY * l2, 0.0)
        orows[f][pl.ds(8 * r * g + j, 8, stride=r)] = x + tend
        return weights[g] * tend

    def wetness(f, g, j):
        return level_of + 8.0 * g.astype(jnp.float32) < faces[f, 1 + j]

    totals = [[None] * r, [None] * r]
    none = jnp.zeros((8, LANES), jnp.float32)
    for f in range(2):

        def inside(g, carry, f=f):
            x = [vrows[f][pl.ds(8 * r * g + j, 8, stride=r)] for j in range(r)]
            wet = {j: wetness(f, g, j) for j in range(1, r - 1)}
            l1 = {}
            for j in range(1, r - 1):
                l1[j] = jnp.where(wet[j], cross(x[j], x[j + 1], x[j - 1]), 0.0)
            for i, j in enumerate((1, 2, r - 3, r - 2)):
                keep[f, g, i] = l1[j]
            return tuple(
                carry[j - 2] + tendency(f, g, j, x[j], l1[j - 1], l1[j], l1[j + 1], wet[j]) for j in range(2, r - 2))

        totals[f][2:r - 2] = lax.fori_loop(0, groups, inside, (none,) * (r - 4), unroll=INNER)

    arrived(COUNT)

    @pl.when(lat > 0)
    def _():
        arrived(NORTHWARD)

    @pl.when(lat < nlat - 1)
    def _():
        arrived(SOUTHWARD)

    counts[0:8] = count_south[...].astype(jnp.float32)
    counts[8 + r:16 + r] = count_north[...].astype(jnp.float32)
    face_rows(-1, -1)
    face_rows(r - 1, r)
    for f in range(2):

        def border(g, carry, f=f):
            x = {j: vrows[f][pl.ds(8 * r * g + j, 8, stride=r)] for j in (0, 1, r - 2, r - 1)}
            for j, at in ((-2, 6), (-1, 7), (r, 0), (r + 1, 1)):
                x[j] = frows[f][pl.ds(64 * g + at, 8, stride=8)]
            wet = {j: wetness(f, g, j) for j in (-1, 0, 1, r - 2, r - 1, r)}
            l1 = {j: keep[f, g, i] for i, j in enumerate((1, 2, r - 3, r - 2))}
            for j in (-1, 0, r - 1, r):
                l1[j] = jnp.where(wet[j], cross(x[j], x[j + 1], x[j - 1]), 0.0)
            return tuple(
                carry[i] + tendency(f, g, j, x[j], l1[j - 1], l1[j], l1[j + 1], wet[j])
                for i, j in enumerate((0, 1, r - 2, r - 1)))

        found = lax.fori_loop(0, groups, border, (none,) * 4, unroll=INNER)
        for i, j in enumerate((0, 1, r - 2, r - 1)):
            totals[f][j] = found[i]
    sub16 = sub_of(zero)
    def stacked(rows_of):
        acc = zero
        for j in range(r):
            acc = jnp.where(sub16 == j, jnp.sum(rows_of[j], 0, keepdims=True), acc)
        return acc

    sum_e, sum_n = stacked(totals[0]), stacked(totals[1])
    half, middle = r // 2, LANES // 2
    scale = TIMESTEP / NSUB
    x, y = scale * sum_e, scale * sum_n
    west_side = jnp.where(slot16 < HALO, x, lanes(y, HALO))
    east_side = jnp.where(slot16 < HALO, lanes(x, HALO), lanes(y, 2 * HALO))
    near = slot16[:half] < middle
    force_out[0] = jnp.where(near, west_side[:half], lanes(west_side[half:], middle))
    force_out[1] = jnp.where(near, east_side[:half], lanes(east_side[half:], middle))
    for o in [0] + offsets:
        part = pl.ds((centre - o) * half, half)
        push(FORCE, force_out.at[1], force_in.at[1, part], 1, o)
        push(FORCE, force_out.at[0], force_in.at[0, part], -1, o)

    force[0, own] = x
    force[1, own] = y
    for o in offsets:
        push(FORCE, force.at[:, own], force.at[:, rows(o)], 0, o)

    def far_column(at):
        return lambda f, g: frows[f][pl.ds(64 * g + at, 8, stride=8)]

    for j, at in ((-2, 6), (-1, 7), (r, 0), (r + 1, 1)):
        strip[2 + j] = gathered(j, far_column(at))
    arrived(EDGE)

    def unpacked(x, side, odd):
        return lanes(x, -HALF if side else HALF) if odd else x

    level_at = (SLOT * (slot % (LANES // SLOT // 2)) + sub).astype(jnp.float32)
    weight = jnp.zeros((8, LANES), jnp.float32)
    for g in range(groups):
        weight = jnp.where(slot % (LANES // SLOT // 2) == g, weights[g], weight)
    drops = []
    for side in range(2):
        source = from_west if side else from_east
        cells = []
        for j in range(-2, r + 2):
            if j < 0:
                far = unpacked(corner_in[2 * side + 1], side, j == -1)
            elif j >= r:
                far = unpacked(corner_in[2 * side], side, j == r + 1)
            else:
                far = unpacked(source[j // 2], side, j % 2)
            cells.append(jnp.where(start, far, strip[2 + j]) if side else jnp.where(start, strip[2 + j], far))
        wet, l1 = [], []
        for j in range(-1, r + 1):
            c = cells[2 + j]
            fe, fn = jnp.minimum(c, lanes(c, -1)), jnp.minimum(c, cells[3 + j])
            f = jnp.where(slot == 0, lanes(fe, -SLOT * groups), jnp.where(slot == SLOT, lanes(fn, SLOT * (SLOT - groups)), 0.0))
            for step in (SLOT, 2 * SLOT, 4 * SLOT):
                f = f + lanes(f, step)
            if side == 0 and 0 <= j < r:
                own_face = jnp.where(lane == LANES - 1, lanes(f, LANES - HALF), faces[0, 1 + j])
                small[5, j:j + 1] = own_face[:1]
                small[6, j:j + 1] = faces[1, 1 + j, 0:1]
            wet.append(level_at < f)
            l1.append(jnp.where(wet[-1], cross(c, cells[3 + j], cells[1 + j]), 0.0))
        drops.append([
            jnp.where(wet[1 + j], -VISCOSITY * cross(l1[1 + j], l1[2 + j], l1[j]), 0.0) for j in range(r)])
    found = []
    for side in range(2):
        x = stacked([weight * d for d in drops[side]])
        for step in (SLOT, 2 * SLOT, 4 * SLOT):
            x = x + lanes(x, -step)
        found.append(x)
    rim16 = (slot16 < 2) | (slot16 >= LANES - 2)
    at_start = slot16 < 2
    sum_e = jnp.where(rim16, jnp.where(at_start, lanes(found[1], -HALF), lanes(found[0], -HALF)), sum_e)
    sum_n = jnp.where(rim16, jnp.where(at_start, lanes(found[1], -HALF - middle), lanes(found[0], -HALF - middle)), sum_n)
    ends = scale * jnp.where(slot16 % middle < SLOT, found[1], lanes(found[0], SLOT))
    mine = pl.ds(centre * half, half)
    seam[mine] = jnp.where(slot16[:half] % middle < 2 * SLOT, ends[:half], lanes(ends[half:], 2 * SLOT))
    for o in offsets:
        push(FORCE, seam.at[mine], seam.at[pl.ds((centre - o) * half, half)], 0, o)
    rim = (lane < 2) | (lane >= LANES - 2)
    for j in range(r):
        ends = jnp.where(start, drops[0][j], drops[1][j])
        for f in range(2):
            for g in range(groups):
                at = pl.ds(8 * r * g + j, 8, stride=r)
                orows[f][at] = jnp.where(
                    rim, vrows[f][at] + lanes(ends, -SLOT * (SLOT * f + g) - HALF), orows[f][at])
    force_tail(tiles, centre, r, arrived, scale * sum_e, scale * sum_n, column_e + sum_e, column_n + sum_n,
               state, side_in, force, force_in, seam, plan, small)
    settle(sum(arriving) - arriving[SOUTHWARD] - arriving[NORTHWARD], send.at[0])

    @pl.when(lat > 0)
    def _():
        settle(arriving[SOUTHWARD], send.at[1])

    @pl.when(lat < nlat - 1)
    def _():
        settle(arriving[NORTHWARD], send.at[2])


INNER = 5


def force_tail(tiles, centre, r, arrived, sum_e, sum_n, column_e, column_n, state, side_in, force, force_in, seam, plan, small):
    span = tiles * r
    nv = span // 8
    own = pl.ds(centre * r, r)
    half = r // 2
    middle = LANES // 2
    lane = lane_of(sum_e)
    arrived(STATE)

    wide = lax.broadcasted_iota(jnp.int32, (span, LANES), 1)
    at_west, at_east = wide < HALO, wide >= LANES - HALO

    def blocks(mine, east, west, f):
        a = jnp.where(at_west, lanes(west, -HALO * f), lanes(mine, HALO))
        b = jnp.where(at_east, lanes(east, -HALO - HALO * f), lanes(mine, -HALO))
        return a, b

    def gate(depth, flux):
        return jnp.where(depth > 0, TIMESTEP * flux, 0.0)

    def divergence(x, y):
        return (x - lanes(x, 1)) + (y - down(y))

    def apply(m, x):
        mc, ae, aw, an, as_ = m
        return mc * x + (ae * lanes(x, -1) + aw * lanes(x, 1)) + (an * up(x) + as_ * down(x))

    square = TIMESTEP * TIMESTEP
    east, west = side_in[0], side_in[1]
    fields = [blocks(state[f], east, west, f) for f in range(4)]
    maps, ones, guess = [], [], []
    for b in range(2):
        d, h, te, tn = [x[b] for x in fields]
        de, dn = jnp.minimum(d, lanes(d, -1)), jnp.minimum(d, up(d))
        ae, an = square * de, square * dn
        aw, as_ = lanes(ae, 1), down(an)
        mc = 2.0 - ((ae + aw) + (an + as_))
        maps.append((mc, ae, aw, an, as_))
        h1 = h - divergence(gate(de, te), gate(dn, tn))
        ones.append(h1)
        guess.append(apply(maps[b], h1) - h)
        for i, x in enumerate((
            mc * mc + ((ae * ae + aw * aw) + (an * an + as_ * as_)) - 2.0,
            ae * (mc + lanes(mc, -1)), aw * (mc + lanes(mc, 1)), an * (mc + up(mc)), as_ * (mc + down(mc)),
            ae * lanes(ae, -1), aw * lanes(aw, 1), an * up(an), as_ * down(as_),
            ae * lanes(an, -1) + an * up(ae), ae * lanes(as_, -1) + as_ * down(ae),
            aw * lanes(an, 1) + an * up(aw), aw * lanes(as_, 1) + as_ * down(aw),
            h,
        )):
            plan[b, i] = x
    depth_own = state[0, own]
    over = state[0, pl.ds(((centre + 1) % tiles) * r, 8)]
    sub = sub_of(depth_own)
    depth_n = jnp.minimum(depth_own, jnp.where(
        sub == r - 1, pltpu.roll(jnp.concatenate([over] * (r // 8), 0), r - 1, 0), up(depth_own)))
    depth_e = jnp.minimum(depth_own, jnp.where(lane == LANES - 1, lanes(side_in[0, own], -1), lanes(depth_own, -1)))
    start_e, start_n = gate(depth_e, state[2, own]), gate(depth_n, state[3, own])

    arrived(FORCE)

    def unfold(x, turn):
        cuts = [x[t * half:t * half + half] for t in range(tiles)]
        return jnp.concatenate([y for c in cuts for y in (c, lanes(c, turn))], 0)

    east, west, ends = unfold(force_in[0], middle), unfold(force_in[1], middle), unfold(seam[...], -2 * SLOT)
    rim_a = (wide >= HALO - 2) & (wide < HALO + 2)
    rim_b = (wide >= LANES - HALO - 2) & (wide < LANES - HALO + 2)
    sides = []
    for f in range(2):
        a, b = blocks(force[f], east, west, f)
        a = jnp.where(rim_a, lanes(ends, HALO - HALF - middle * f), a)
        b = jnp.where(rim_b, lanes(ends, LANES - HALO - HALF - SLOT - middle * f), b)
        sides.append((a, b))
    fe, fn = sides
    drift = [divergence(fe[b], fn[b]) for b in range(2)]
    for b in range(2):
        plan[b, 14] = guess[b] - drift[b]
        plan[b, 15] = apply(maps[b], drift[b]) + 2.0 * drift[b]

    def dealt(b, i):
        return jnp.concatenate([plan[b, i, pl.ds(v, 8, stride=nv)] for v in range(nv)], 0)

    def next_row(x):
        return jnp.concatenate([x[8:], pltpu.roll(x[:8], 7, 0)], 0)

    def prior_row(x):
        return jnp.concatenate([pltpu.roll(x[span - 8:], 1, 0), x[:span - 8]], 0)

    pairs = NSUB // 2
    odd = [0] * (pairs + 1)
    for k in reversed(range(pairs)):
        odd[k] = NSUB - 2 * k - odd[k + 1]
    fixed = [[dealt(b, i) for i in range(13)] for b in range(2)]
    push_by = [dealt(b, 15) for b in range(2)]
    before = [dealt(b, 13) for b in range(2)]
    now = [dealt(b, 14) for b in range(2)]
    all_sum = [(NSUB - 1.0) * x for x in now]
    odd_sum = [float(odd[1]) * x for x in now]
    for k in range(2, pairs + 1):
        for b in range(2):
            h = now[b]
            c, e, w, n, s, ee, ww, nn, ss, en, es, wn, ws = fixed[b]
            he, hw, hn, hs = lanes(h, -1), lanes(h, 1), next_row(h), prior_row(h)
            core = (c * h - (before[b] + push_by[b])) + ((n * hn + s * hs) + (nn * next_row(hn) + ss * prior_row(hs)))
            side = (e * he + (en * next_row(he) + es * prior_row(he))) + (w * hw + (wn * next_row(hw) + ws * prior_row(hw)))
            before[b], now[b] = h, core + (side + (ee * lanes(h, -2) + ww * lanes(h, 2)))
            if k < pairs:
                odd_sum[b] += float(odd[k]) * now[b]
            all_sum[b] += (NSUB + 1.0 - 2 * k) * now[b]
    for b in range(2):
        for i, x in ((0, now[b]), (1, all_sum[b]), (2, odd_sum[b])):
            for v in range(nv):
                plan[b, i, pl.ds(v, 8, stride=nv)] = x[8 * v:8 * v + 8]

    left = lane < middle
    at = 8 if tiles >= 3 else centre * r
    low, size = (centre * r - 8, r + 16) if tiles >= 3 else (0, span)
    ends, here, easts, norths = [], [], [], []
    for b in range(2):
        m = [x[low:low + size] for x in maps[b]]
        total = (plan[b, 1, pl.ds(low, size)] + (odd[0] * ones[b][low:low + size] - float(sum(odd[1:])) * drift[b][low:low + size])
                 + apply(m, plan[b, 2, pl.ds(low, size)]))
        ends.append(plan[b, 0, own])
        here.append(total[at:at + r])
        easts.append(lanes(total, -1)[at:at + r])
        norths.append(up(total)[at:at + r])

    def joined(x):
        return jnp.where(left, lanes(x[0], -HALO), lanes(x[1], HALO))

    u, u_east, u_north = joined(here), joined(easts), joined(norths)
    ramp = NSUB * (NSUB + 1) / 2
    total_e = NSUB * start_e - square * depth_e * (u_east - u) + ramp * sum_e
    total_n = NSUB * start_n - square * depth_n * (u_north - u) + ramp * sum_n
    mean_e = total_e / (NSUB * TIMESTEP)
    mean_n = total_n / (NSUB * TIMESTEP)
    one = jnp.ones((r, LANES), jnp.float32)
    small[0] = joined(ends)
    small[1] = mean_e
    small[2] = mean_n
    small[3] = (mean_e - column_e) / (depth_e + jnp.where(depth_e > 0, 0.0, one))
    small[4] = (mean_n - column_n) / (depth_n + jnp.where(depth_n > 0, 0.0, one))


def finish(after_e, after_n, small, oe, on, oh, ome, omn):
    oh[...] = small[0]
    ome[...] = small[1]
    omn[...] = small[2]
    face_e, face_n = small[5], small[6]
    shift_e, shift_n = small[3], small[4]

    def level(k, _):
        depth = k.astype(jnp.float32)
        oe[k] = jnp.where(depth < face_e, after_e[k] + shift_e, 0.0)
        on[k] = jnp.where(depth < face_n, after_n[k] + shift_n, 0.0)
        return 0

    lax.fori_loop(0, after_e.shape[0], level, 0, unroll=4)


def solution(mesh):
    nlon, nlat = mesh.shape["lon"], mesh.shape["lat"]

    def shards(ve, vn, cnt, height, te, tn, thick):
        layers, r, width = ve.shape
        reach = -(-NSUB // r)
        tiles = min(nlat, 2 * reach + 1)
        centre = tiles // 2
        span = tiles * r
        groups = layers // 8
        f32, i32 = jnp.float32, jnp.int32
        tile = (r, width)
        vm = pltpu.VMEM
        vspec = pl.BlockSpec(memory_space=pltpu.VMEM)
        after_e, after_n, small = pl.pallas_call(
            functools.partial(kernel, nlon, nlat, tiles, centre),
            out_shape=(
                jax.ShapeDtypeStruct(ve.shape, f32),
                jax.ShapeDtypeStruct(ve.shape, f32),
                jax.ShapeDtypeStruct((7, *tile), f32),
            ),
            in_specs=[pl.BlockSpec(memory_space=pltpu.HBM)] * 7,
            out_specs=[vspec] * 3,
            scratch_shapes=[
                pltpu.SMEM((layers,), f32),
                vm(ve.shape, f32),
                vm(ve.shape, f32),
                vm(tile, i32),
                pltpu.SemaphoreType.DMA((5,)),
                vm((layers, 8, width), f32),
                vm((layers, 8, width), f32),
                vm((2, r // 2, 8, width), f32),
                vm((r // 2, 8, width), f32),
                vm((r // 2, 8, width), f32),
                vm((4, 8, width), f32),
                vm((r + 4, 8, width), f32),
                vm((2, r + 2, 8, width), f32),
                vm((2, groups, 4, 8, width), f32),
                vm((groups, 8, width), f32),
                vm((r + 16, width), f32),
                vm((8, width), i32),
                vm((8, width), i32),
                vm((4, span, width), f32),
                vm((2, *tile), f32),
                vm((2, span, width), f32),
                vm((2, span, width), f32),
                vm((2, r // 2, width), f32),
                vm((2, span // 2, width), f32),
                vm((span // 2, width), f32),
                vm((2, 17, span, width), f32),
                pltpu.SemaphoreType.DMA((3,)),
                pltpu.SemaphoreType.DMA((6,)),
            ],
            compiler_params=pltpu.CompilerParams(
                collective_id=0, has_side_effects=True, vmem_limit_bytes=16 << 20),
        )(*[pltpu.with_memory_space_constraint(x, pltpu.HBM) for x in (thick, ve, vn, cnt, height, te, tn)])
        out = jax.ShapeDtypeStruct(tile, f32)
        levels = jax.ShapeDtypeStruct(ve.shape, f32)
        return pl.pallas_call(
            finish,
            out_shape=(levels, levels, out, out, out),
            in_specs=[vspec] * 3,
            out_specs=[vspec] * 5,
            compiler_params=pltpu.CompilerParams(vmem_limit_bytes=16 << 20),
        )(after_e, after_n, small)

    level = P(None, "lat", "lon")
    flat = P("lat", "lon")
    return jax.shard_map(
        shards,
        mesh=mesh,
        in_specs=(level, level, flat, flat, flat, flat, P()),
        out_specs=(level, level, flat, flat, flat),
        check_vma=False,
    )
```

```python
import functools
import math

import jax
import jax.numpy as jnp
from jax import lax
from jax.experimental import pallas as pl
from jax.experimental.pallas import tpu as pltpu
from jax.sharding import PartitionSpec as P

NSUB = 30
VISCOSITY = 0.01
TIMESTEP = 0.35
LANES = 128
SLOT = 8
HALF = SLOT // 2
HALO = 32
MESH = pl.DeviceIdType.MESH
COUNT, EDGE, SOUTHWARD, NORTHWARD, STATE, FORCE = range(6)


def lane_of(x):
    return lax.broadcasted_iota(jnp.int32, x.shape, 1)


def sub_of(x):
    return lax.broadcasted_iota(jnp.int32, x.shape, 0)


def lanes(x, shift):
    return pltpu.roll(x, shift % LANES, 1) if shift % LANES else x


def up(x):
    return pltpu.roll(x, x.shape[0] - 1, 0)


def down(x):
    return pltpu.roll(x, 1, 0)


def merge(parts, lane):
    bit = SLOT
    while len(parts) > 1:
        odd = lane // bit % 2 == 1
        pairs = [(parts[i], parts[i + 1]) for i in range(0, len(parts), 2)]
        parts = [b if a is None else a if b is None else jnp.where(odd, b, a) for a, b in pairs]
        bit *= 2
    return parts[0]


def kernel(
    nlon, nlat, tiles, centre,
    thick_hbm, ve_hbm, vn_hbm, cnt_hbm, height_hbm, te_hbm, tn_hbm,
    oe, on, small,
    thick, ve, vn, cnt, loads,
    rows_e, rows_n, edges, from_east, from_west, corner_in, strip, faces, keep, weights, counts,
    count_north, count_south,
    state, side_out, side_in, force, force_out, force_in, seam, plan,
    send, recv, knock,
):
    layers, r, _ = ve.shape
    groups = layers // 8
    lon, lat = lax.axis_index("lon"), lax.axis_index("lat")
    offsets = [o for o in range(centre - tiles + 1, centre + 1) if o != 0]
    own = pl.ds(centre * r, r)

    def device(dx, dy):
        return {"lon": lax.rem(lon + nlon + dx, nlon), "lat": lax.rem(lat + nlat + dy, nlat)}

    partners = [(0, o) for o in offsets] + [(-1, o) for o in [0] + offsets]
    barrier = pltpu.get_barrier_semaphore()
    for dx, dy in partners:
        pl.semaphore_signal(barrier, inc=1, device_id=device(dx, dy), device_id_type=MESH)

    @pl.when(lon < nlon - 1)
    def _():
        for o in [0] + offsets:
            pl.semaphore_signal(barrier, inc=1, device_id=device(1, o), device_id_type=MESH)

    fetched = []
    for i, far, near in (
        (0, ve_hbm, ve), (1, vn_hbm, vn), (2, cnt_hbm, cnt), (3, thick_hbm, thick),
        (4, height_hbm, state.at[1, own]), (4, te_hbm, state.at[2, own]), (4, tn_hbm, state.at[3, own]),
    ):
        fetched.append(pltpu.make_async_copy(far, near, loads.at[i]))
        fetched[-1].start()

    blank = plan.reshape(plan.shape[0] * plan.shape[1] * plan.shape[2], LANES)
    arriving = [0] * recv.shape[0]

    def sender(kind):
        return {SOUTHWARD: 1, NORTHWARD: 2}.get(kind, 0)

    def push(kind, src, dst, dx, dy, again=False):
        pltpu.make_async_remote_copy(
            src_ref=src, dst_ref=dst, send_sem=send.at[sender(kind)], recv_sem=recv.at[kind],
            device_id=device(dx, dy), device_id_type=MESH).start()
        arriving[kind] += 0 if again else math.prod(dst.shape) // LANES

    def settle(rows, sem):
        part = blank.at[pl.ds(0, rows)]
        pltpu.make_async_copy(part, part, sem).wait()

    def arrived(kind):
        settle(arriving[kind], recv.at[kind])

    low8, high8 = pl.ds(0, 8), pl.ds(r - 8, 8)
    @pl.when(lon > 0)
    def _():
        pl.semaphore_wait(barrier, len(partners) + tiles)

    @pl.when(lon == 0)
    def _():
        pl.semaphore_wait(barrier, len(partners))

    @pl.when(lon == nlon - 1)
    def _():
        for o in [0] + offsets:
            pl.semaphore_signal(knock, inc=1, device_id=device(1, o), device_id_type=MESH)

    @pl.when(lat > 0)
    def _():
        for v, buf in ((ve_hbm, rows_e), (vn_hbm, rows_n)):
            push(SOUTHWARD, v.at[:, pl.ds(0, 2)], buf.at[:, pl.ds(0, 2)], 0, -1)

    @pl.when(lat < nlat - 1)
    def _():
        for v, buf in ((ve_hbm, rows_e), (vn_hbm, rows_n)):
            push(NORTHWARD, v.at[:, pl.ds(r - 2, 2)], buf.at[:, pl.ds(6, 2)], 0, 1)

    push(COUNT, cnt_hbm.at[low8], count_north, 0, -1)
    push(COUNT, cnt_hbm.at[high8], count_south, 0, 1)

    for c in fetched[:4]:
        c.wait()

    vrows = [v.reshape(layers * r, LANES) for v in (ve, vn)]
    frows = [v.reshape(layers * 8, LANES) for v in (rows_e, rows_n)]
    orows = [v.reshape(layers * r, LANES) for v in (oe, on)]
    lane = lax.broadcasted_iota(jnp.int32, (8, LANES), 1)
    sub = lax.broadcasted_iota(jnp.int32, (8, LANES), 0)
    slot = lane // SLOT
    start = lane % SLOT < HALF

    cnt_own = cnt[...]
    counts[8:8 + r] = cnt_own.astype(jnp.float32)

    def spread_row(j):
        return jnp.broadcast_to(counts[8 + j:9 + j], (8, LANES))

    def gathered(j, column):
        parts = [None] * (LANES // SLOT)
        for f in range(2):
            for g in range(groups):
                parts[LANES // SLOT // 2 * f + g] = column(f, g)
        parts[groups] = spread_row(j)
        parts = [None if x is None else lanes(x, SLOT * i + HALF) for i, x in enumerate(parts)]
        return merge(parts, lane)

    def own_column(j):
        return lambda f, g: vrows[f][pl.ds(8 * g * r + j, 8, stride=r)]

    for j in range(r):
        strip[2 + j] = gathered(j, own_column(j))
    for i in range(r // 2):
        a, b = strip[2 + 2 * i], strip[3 + 2 * i]
        edges[0, i] = jnp.where(start, lanes(b, -HALF), a)
        edges[1, i] = jnp.where(start, a, lanes(b, HALF))
    push(EDGE, edges.at[1], from_west, 1, 0)
    for dy, at, i in ((-1, 2, 0), (1, 3, r // 2 - 1)):
        push(EDGE, edges.at[1, i], corner_in.at[at], 1, dy)

    def edges_west(again):
        push(EDGE, edges.at[0], from_east, -1, 0, again)
        for dy, at, i in ((-1, 0, 0), (1, 1, r // 2 - 1)):
            push(EDGE, edges.at[0, i], corner_in.at[at], -1, dy, again)

    @pl.when(lon > 0)
    def _():
        edges_west(False)

    zero = jnp.zeros((r, LANES), jnp.float32)

    def deepen(k, d):
        return jnp.where(k < cnt_own, d + thick[k], d)

    depth = lax.fori_loop(0, layers, deepen, zero, unroll=8)
    state[0, own] = depth
    pltpu.make_async_copy(state.at[pl.ds(1, 3), own], state.at[pl.ds(1, 3), own], loads.at[4]).wait()
    four = [depth] + [state[f, own] for f in range(1, 4)]
    slot16 = lane_of(depth)
    west_side, east_side = four[0], lanes(four[0], HALO)
    for f in range(1, 4):
        here = slot16 // HALO == f
        west_side = jnp.where(here, lanes(four[f], HALO * f), west_side)
        east_side = jnp.where(here, lanes(four[f], HALO * f + HALO), east_side)
    side_out[0] = west_side
    side_out[1] = east_side

    def rows(o):
        return pl.ds((centre - o) * r, r)

    for o in [0] + offsets:
        push(STATE, side_out.at[1], side_in.at[1, rows(o)], 1, o)

    def state_west(again):
        for o in [0] + offsets:
            push(STATE, side_out.at[0], side_in.at[0, rows(o)], -1, o, again)

    @pl.when(lon > 0)
    def _():
        state_west(False)

    for o in offsets:
        push(STATE, state.at[:, own], state.at[:, rows(o)], 0, o)

    def columns(k, carry):
        a, b = carry
        return a + thick[k] * ve[k], b + thick[k] * vn[k]

    column_e, column_n = lax.fori_loop(0, layers, columns, (zero, zero), unroll=8)
    for g in range(groups):
        w = jnp.zeros((8, LANES), jnp.float32)
        for i in range(8):
            w = jnp.where(sub == i, thick[8 * g + i], w)
        weights[g] = w

    def face_rows(low, high):
        here = [spread_row(j) for j in range(low, high + 2)]
        for i, j in enumerate(range(low, high + 1)):
            c = here[i]
            faces[0, 1 + j] = jnp.minimum(c, lanes(c, -1))
            faces[1, 1 + j] = jnp.minimum(c, here[i + 1])

    face_rows(0, r - 2)
    level_of = sub.astype(jnp.float32)

    def cross(x, n, s):
        return (lanes(x, -1) + lanes(x, 1)) + (n + s) - 4.0 * x

    def tendency(f, g, j, x, low, mid, high, wet):
        l2 = cross(mid, high, low)
        tend = jnp.where(wet, -VISCOSITY * l2, 0.0)
        orows[f][pl.ds(8 * r * g + j, 8, stride=r)] = x + tend
        return weights[g] * tend

    def wetness(f, g, j):
        return level_of + 8.0 * g.astype(jnp.float32) < faces[f, 1 + j]

    totals = [[None] * r, [None] * r]
    none = jnp.zeros((8, LANES), jnp.float32)
    for f in range(2):

        def inside(g, carry, f=f):
            x = [vrows[f][pl.ds(8 * r * g + j, 8, stride=r)] for j in range(r)]
            wet = {j: wetness(f, g, j) for j in range(1, r - 1)}
            l1 = {}
            for j in range(1, r - 1):
                l1[j] = jnp.where(wet[j], cross(x[j], x[j + 1], x[j - 1]), 0.0)
            for i, j in enumerate((1, 2, r - 3, r - 2)):
                keep[f, g, i] = l1[j]
            return tuple(
                carry[j - 2] + tendency(f, g, j, x[j], l1[j - 1], l1[j], l1[j + 1], wet[j]) for j in range(2, r - 2))

        totals[f][2:r - 2] = lax.fori_loop(0, groups, inside, (none,) * (r - 4), unroll=INNER)

    arrived(COUNT)

    @pl.when(lat > 0)
    def _():
        arrived(NORTHWARD)

    @pl.when(lat < nlat - 1)
    def _():
        arrived(SOUTHWARD)

    counts[0:8] = count_south[...].astype(jnp.float32)
    counts[8 + r:16 + r] = count_north[...].astype(jnp.float32)
    face_rows(-1, -1)
    face_rows(r - 1, r)
    for f in range(2):

        def border(g, carry, f=f):
            x = {j: vrows[f][pl.ds(8 * r * g + j, 8, stride=r)] for j in (0, 1, r - 2, r - 1)}
            for j, at in ((-2, 6), (-1, 7), (r, 0), (r + 1, 1)):
                x[j] = frows[f][pl.ds(64 * g + at, 8, stride=8)]
            wet = {j: wetness(f, g, j) for j in (-1, 0, 1, r - 2, r - 1, r)}
            l1 = {j: keep[f, g, i] for i, j in enumerate((1, 2, r - 3, r - 2))}
            for j in (-1, 0, r - 1, r):
                l1[j] = jnp.where(wet[j], cross(x[j], x[j + 1], x[j - 1]), 0.0)
            return tuple(
                carry[i] + tendency(f, g, j, x[j], l1[j - 1], l1[j], l1[j + 1], wet[j])
                for i, j in enumerate((0, 1, r - 2, r - 1)))

        found = lax.fori_loop(0, groups, border, (none,) * 4, unroll=INNER)
        for i, j in enumerate((0, 1, r - 2, r - 1)):
            totals[f][j] = found[i]
    sub16 = sub_of(zero)
    def stacked(rows_of):
        acc = zero
        for j in range(r):
            acc = jnp.where(sub16 == j, jnp.sum(rows_of[j], 0, keepdims=True), acc)
        return acc

    sum_e, sum_n = stacked(totals[0]), stacked(totals[1])
    half, middle = r // 2, LANES // 2
    scale = TIMESTEP / NSUB
    x, y = scale * sum_e, scale * sum_n
    west_side = jnp.where(slot16 < HALO, x, lanes(y, HALO))
    east_side = jnp.where(slot16 < HALO, lanes(x, HALO), lanes(y, 2 * HALO))
    front = slot16[:half] < middle
    force_out[0] = jnp.where(front, west_side[:half], lanes(west_side[half:], middle))
    force_out[1] = jnp.where(front, east_side[:half], lanes(east_side[half:], middle))
    def part(o):
        return pl.ds((centre - o) * half, half)

    for o in [0] + offsets:
        push(FORCE, force_out.at[1], force_in.at[1, part(o)], 1, o)

    def force_west(again):
        for o in [0] + offsets:
            push(FORCE, force_out.at[0], force_in.at[0, part(o)], -1, o, again)

    @pl.when(lon > 0)
    def _():
        force_west(False)

    force[0, own] = x
    force[1, own] = y
    for o in offsets:
        push(FORCE, force.at[:, own], force.at[:, rows(o)], 0, o)

    def far_column(at):
        return lambda f, g: frows[f][pl.ds(64 * g + at, 8, stride=8)]

    for j, at in ((-2, 6), (-1, 7), (r, 0), (r + 1, 1)):
        strip[2 + j] = gathered(j, far_column(at))
    @pl.when(lon == 0)
    def _():
        pl.semaphore_wait(knock, tiles)
        edges_west(True)
        state_west(True)
        force_west(True)

    arrived(EDGE)


    def unpacked(x, side, odd):
        return lanes(x, -HALF if side else HALF) if odd else x

    level_at = (SLOT * (slot % (LANES // SLOT // 2)) + sub).astype(jnp.float32)
    weight = jnp.zeros((8, LANES), jnp.float32)
    for g in range(groups):
        weight = jnp.where(slot % (LANES // SLOT // 2) == g, weights[g], weight)
    drops = []
    for side in range(2):
        source = from_west if side else from_east
        cells = []
        for j in range(-2, r + 2):
            if j < 0:
                far = unpacked(corner_in[2 * side + 1], side, j == -1)
            elif j >= r:
                far = unpacked(corner_in[2 * side], side, j == r + 1)
            else:
                far = unpacked(source[j // 2], side, j % 2)
            cells.append(jnp.where(start, far, strip[2 + j]) if side else jnp.where(start, strip[2 + j], far))
        wet, l1 = [], []
        for j in range(-1, r + 1):
            c = cells[2 + j]
            fe, fn = jnp.minimum(c, lanes(c, -1)), jnp.minimum(c, cells[3 + j])
            f = jnp.where(slot == 0, lanes(fe, -SLOT * groups), jnp.where(slot == SLOT, lanes(fn, SLOT * (SLOT - groups)), 0.0))
            for step in (SLOT, 2 * SLOT, 4 * SLOT):
                f = f + lanes(f, step)
            if side == 0 and 0 <= j < r:
                own_face = jnp.where(lane == LANES - 1, lanes(f, LANES - HALF), faces[0, 1 + j])
                small[5, j:j + 1] = own_face[:1]
                small[6, j:j + 1] = faces[1, 1 + j, 0:1]
            wet.append(level_at < f)
            l1.append(jnp.where(wet[-1], cross(c, cells[3 + j], cells[1 + j]), 0.0))
        drops.append([
            jnp.where(wet[1 + j], -VISCOSITY * cross(l1[1 + j], l1[2 + j], l1[j]), 0.0) for j in range(r)])
    found = []
    for side in range(2):
        x = stacked([weight * d for d in drops[side]])
        for step in (SLOT, 2 * SLOT, 4 * SLOT):
            x = x + lanes(x, -step)
        found.append(x)
    rim16 = (slot16 < 2) | (slot16 >= LANES - 2)
    at_start = slot16 < 2
    sum_e = jnp.where(rim16, jnp.where(at_start, lanes(found[1], -HALF), lanes(found[0], -HALF)), sum_e)
    sum_n = jnp.where(rim16, jnp.where(at_start, lanes(found[1], -HALF - middle), lanes(found[0], -HALF - middle)), sum_n)
    ends = scale * jnp.where(slot16 % middle < SLOT, found[1], lanes(found[0], SLOT))
    mine = pl.ds(centre * half, half)
    seam[mine] = jnp.where(slot16[:half] % middle < 2 * SLOT, ends[:half], lanes(ends[half:], 2 * SLOT))
    for o in offsets:
        push(FORCE, seam.at[mine], seam.at[part(o)], 0, o)
    rim = (lane < 2) | (lane >= LANES - 2)
    for j in range(r):
        ends = jnp.where(start, drops[0][j], drops[1][j])
        for f in range(2):
            for g in range(groups):
                at = pl.ds(8 * r * g + j, 8, stride=r)
                orows[f][at] = jnp.where(
                    rim, vrows[f][at] + lanes(ends, -SLOT * (SLOT * f + g) - HALF), orows[f][at])
    force_tail(tiles, centre, r, arrived, scale * sum_e, scale * sum_n, column_e + sum_e, column_n + sum_n,
               state, side_in, force, force_in, seam, plan, small)
    settle(sum(arriving) - arriving[SOUTHWARD] - arriving[NORTHWARD], send.at[0])

    @pl.when(lat > 0)
    def _():
        settle(arriving[SOUTHWARD], send.at[1])

    @pl.when(lat < nlat - 1)
    def _():
        settle(arriving[NORTHWARD], send.at[2])


INNER = 5


def force_tail(tiles, centre, r, arrived, sum_e, sum_n, column_e, column_n, state, side_in, force, force_in, seam, plan, small):
    span = tiles * r
    nv = span // 8
    own = pl.ds(centre * r, r)
    half = r // 2
    middle = LANES // 2
    lane = lane_of(sum_e)
    arrived(STATE)

    wide = lax.broadcasted_iota(jnp.int32, (span, LANES), 1)
    at_west, at_east = wide < HALO, wide >= LANES - HALO

    def blocks(mine, east, west, f):
        a = jnp.where(at_west, lanes(west, -HALO * f), lanes(mine, HALO))
        b = jnp.where(at_east, lanes(east, -HALO - HALO * f), lanes(mine, -HALO))
        return a, b

    def gate(depth, flux):
        return jnp.where(depth > 0, TIMESTEP * flux, 0.0)

    def divergence(x, y):
        return (x - lanes(x, 1)) + (y - down(y))

    def apply(m, x):
        mc, ae, aw, an, as_ = m
        return mc * x + (ae * lanes(x, -1) + aw * lanes(x, 1)) + (an * up(x) + as_ * down(x))

    square = TIMESTEP * TIMESTEP
    east, west = side_in[0], side_in[1]
    fields = [blocks(state[f], east, west, f) for f in range(4)]
    maps, ones, guess = [], [], []
    for b in range(2):
        d, h, te, tn = [x[b] for x in fields]
        de, dn = jnp.minimum(d, lanes(d, -1)), jnp.minimum(d, up(d))
        ae, an = square * de, square * dn
        aw, as_ = lanes(ae, 1), down(an)
        mc = 2.0 - ((ae + aw) + (an + as_))
        maps.append((mc, ae, aw, an, as_))
        h1 = h - divergence(gate(de, te), gate(dn, tn))
        ones.append(h1)
        guess.append(apply(maps[b], h1) - h)
        for i, x in enumerate((
            mc * mc + ((ae * ae + aw * aw) + (an * an + as_ * as_)) - 2.0,
            ae * (mc + lanes(mc, -1)), aw * (mc + lanes(mc, 1)), an * (mc + up(mc)), as_ * (mc + down(mc)),
            ae * lanes(ae, -1), aw * lanes(aw, 1), an * up(an), as_ * down(as_),
            ae * lanes(an, -1) + an * up(ae), ae * lanes(as_, -1) + as_ * down(ae),
            aw * lanes(an, 1) + an * up(aw), aw * lanes(as_, 1) + as_ * down(aw),
            h,
        )):
            plan[b, i] = x
    depth_own = state[0, own]
    over = state[0, pl.ds(((centre + 1) % tiles) * r, 8)]
    sub = sub_of(depth_own)
    depth_n = jnp.minimum(depth_own, jnp.where(
        sub == r - 1, pltpu.roll(jnp.concatenate([over] * (r // 8), 0), r - 1, 0), up(depth_own)))
    depth_e = jnp.minimum(depth_own, jnp.where(lane == LANES - 1, lanes(side_in[0, own], -1), lanes(depth_own, -1)))
    start_e, start_n = gate(depth_e, state[2, own]), gate(depth_n, state[3, own])

    arrived(FORCE)

    def unfold(x, turn):
        cuts = [x[t * half:t * half + half] for t in range(tiles)]
        return jnp.concatenate([y for c in cuts for y in (c, lanes(c, turn))], 0)

    east, west, ends = unfold(force_in[0], middle), unfold(force_in[1], middle), unfold(seam[...], -2 * SLOT)
    rim_a = (wide >= HALO - 2) & (wide < HALO + 2)
    rim_b = (wide >= LANES - HALO - 2) & (wide < LANES - HALO + 2)
    sides = []
    for f in range(2):
        a, b = blocks(force[f], east, west, f)
        a = jnp.where(rim_a, lanes(ends, HALO - HALF - middle * f), a)
        b = jnp.where(rim_b, lanes(ends, LANES - HALO - HALF - SLOT - middle * f), b)
        sides.append((a, b))
    fe, fn = sides
    drift = [divergence(fe[b], fn[b]) for b in range(2)]
    for b in range(2):
        plan[b, 14] = guess[b] - drift[b]
        plan[b, 15] = apply(maps[b], drift[b]) + 2.0 * drift[b]

    def dealt(b, i):
        return jnp.concatenate([plan[b, i, pl.ds(v, 8, stride=nv)] for v in range(nv)], 0)

    def next_row(x):
        return jnp.concatenate([x[8:], pltpu.roll(x[:8], 7, 0)], 0)

    def prior_row(x):
        return jnp.concatenate([pltpu.roll(x[span - 8:], 1, 0), x[:span - 8]], 0)

    pairs = NSUB // 2
    odd = [0] * (pairs + 1)
    for k in reversed(range(pairs)):
        odd[k] = NSUB - 2 * k - odd[k + 1]
    fixed = [[dealt(b, i) for i in range(13)] for b in range(2)]
    push_by = [dealt(b, 15) for b in range(2)]
    before = [dealt(b, 13) for b in range(2)]
    now = [dealt(b, 14) for b in range(2)]
    all_sum = [(NSUB - 1.0) * x for x in now]
    odd_sum = [float(odd[1]) * x for x in now]
    for k in range(2, pairs + 1):
        for b in range(2):
            h = now[b]
            c, e, w, n, s, ee, ww, nn, ss, en, es, wn, ws = fixed[b]
            he, hw, hn, hs = lanes(h, -1), lanes(h, 1), next_row(h), prior_row(h)
            core = (c * h - (before[b] + push_by[b])) + ((n * hn + s * hs) + (nn * next_row(hn) + ss * prior_row(hs)))
            side = (e * he + (en * next_row(he) + es * prior_row(he))) + (w * hw + (wn * next_row(hw) + ws * prior_row(hw)))
            before[b], now[b] = h, core + (side + (ee * lanes(h, -2) + ww * lanes(h, 2)))
            if k < pairs:
                odd_sum[b] += float(odd[k]) * now[b]
            all_sum[b] += (NSUB + 1.0 - 2 * k) * now[b]
    for b in range(2):
        for i, x in ((0, now[b]), (1, all_sum[b]), (2, odd_sum[b])):
            for v in range(nv):
                plan[b, i, pl.ds(v, 8, stride=nv)] = x[8 * v:8 * v + 8]

    left = lane < middle
    at = 8 if tiles >= 3 else centre * r
    low, size = (centre * r - 8, r + 16) if tiles >= 3 else (0, span)
    ends, here, easts, norths = [], [], [], []
    for b in range(2):
        m = [x[low:low + size] for x in maps[b]]
        total = (plan[b, 1, pl.ds(low, size)] + (odd[0] * ones[b][low:low + size] - float(sum(odd[1:])) * drift[b][low:low + size])
                 + apply(m, plan[b, 2, pl.ds(low, size)]))
        ends.append(plan[b, 0, own])
        here.append(total[at:at + r])
        easts.append(lanes(total, -1)[at:at + r])
        norths.append(up(total)[at:at + r])

    def joined(x):
        return jnp.where(left, lanes(x[0], -HALO), lanes(x[1], HALO))

    u, u_east, u_north = joined(here), joined(easts), joined(norths)
    ramp = NSUB * (NSUB + 1) / 2
    total_e = NSUB * start_e - square * depth_e * (u_east - u) + ramp * sum_e
    total_n = NSUB * start_n - square * depth_n * (u_north - u) + ramp * sum_n
    mean_e = total_e / (NSUB * TIMESTEP)
    mean_n = total_n / (NSUB * TIMESTEP)
    one = jnp.ones((r, LANES), jnp.float32)
    small[0] = joined(ends)
    small[1] = mean_e
    small[2] = mean_n
    small[3] = (mean_e - column_e) / (depth_e + jnp.where(depth_e > 0, 0.0, one))
    small[4] = (mean_n - column_n) / (depth_n + jnp.where(depth_n > 0, 0.0, one))


def finish(after_e, after_n, small, oe, on, oh, ome, omn):
    oh[...] = small[0]
    ome[...] = small[1]
    omn[...] = small[2]
    face_e, face_n = small[5], small[6]
    shift_e, shift_n = small[3], small[4]

    def level(k, _):
        depth = k.astype(jnp.float32)
        oe[k] = jnp.where(depth < face_e, after_e[k] + shift_e, 0.0)
        on[k] = jnp.where(depth < face_n, after_n[k] + shift_n, 0.0)
        return 0

    lax.fori_loop(0, after_e.shape[0], level, 0, unroll=4)


def solution(mesh):
    nlon, nlat = mesh.shape["lon"], mesh.shape["lat"]

    def shards(ve, vn, cnt, height, te, tn, thick):
        layers, r, width = ve.shape
        reach = -(-NSUB // r)
        tiles = min(nlat, 2 * reach + 1)
        centre = tiles // 2
        span = tiles * r
        groups = layers // 8
        f32, i32 = jnp.float32, jnp.int32
        tile = (r, width)
        vm = pltpu.VMEM
        vspec = pl.BlockSpec(memory_space=pltpu.VMEM)
        after_e, after_n, small = pl.pallas_call(
            functools.partial(kernel, nlon, nlat, tiles, centre),
            out_shape=(
                jax.ShapeDtypeStruct(ve.shape, f32),
                jax.ShapeDtypeStruct(ve.shape, f32),
                jax.ShapeDtypeStruct((7, *tile), f32),
            ),
            in_specs=[pl.BlockSpec(memory_space=pltpu.HBM)] * 7,
            out_specs=[vspec] * 3,
            scratch_shapes=[
                pltpu.SMEM((layers,), f32),
                vm(ve.shape, f32),
                vm(ve.shape, f32),
                vm(tile, i32),
                pltpu.SemaphoreType.DMA((5,)),
                vm((layers, 8, width), f32),
                vm((layers, 8, width), f32),
                vm((2, r // 2, 8, width), f32),
                vm((r // 2, 8, width), f32),
                vm((r // 2, 8, width), f32),
                vm((4, 8, width), f32),
                vm((r + 4, 8, width), f32),
                vm((2, r + 2, 8, width), f32),
                vm((2, groups, 4, 8, width), f32),
                vm((groups, 8, width), f32),
                vm((r + 16, width), f32),
                vm((8, width), i32),
                vm((8, width), i32),
                vm((4, span, width), f32),
                vm((2, *tile), f32),
                vm((2, span, width), f32),
                vm((2, span, width), f32),
                vm((2, r // 2, width), f32),
                vm((2, span // 2, width), f32),
                vm((span // 2, width), f32),
                vm((2, 17, span, width), f32),
                pltpu.SemaphoreType.DMA((3,)),
                pltpu.SemaphoreType.DMA((6,)),
                pltpu.SemaphoreType.REGULAR,
            ],
            compiler_params=pltpu.CompilerParams(
                collective_id=0, has_side_effects=True, vmem_limit_bytes=16 << 20),
        )(*[pltpu.with_memory_space_constraint(x, pltpu.HBM) for x in (thick, ve, vn, cnt, height, te, tn)])
        out = jax.ShapeDtypeStruct(tile, f32)
        levels = jax.ShapeDtypeStruct(ve.shape, f32)
        return pl.pallas_call(
            finish,
            out_shape=(levels, levels, out, out, out),
            in_specs=[vspec] * 3,
            out_specs=[vspec] * 5,
            compiler_params=pltpu.CompilerParams(vmem_limit_bytes=16 << 20),
        )(after_e, after_n, small)

    level = P(None, "lat", "lon")
    flat = P("lat", "lon")
    return jax.shard_map(
        shards,
        mesh=mesh,
        in_specs=(level, level, flat, flat, flat, flat, P()),
        out_specs=(level, level, flat, flat, flat),
        check_vma=False,
    )
```

```python
import functools
import math

import jax
import jax.numpy as jnp
from jax import lax
from jax.experimental import pallas as pl
from jax.experimental.pallas import tpu as pltpu
from jax.sharding import PartitionSpec as P

NSUB = 30
VISCOSITY = 0.01
TIMESTEP = 0.35
LANES = 128
SLOT = 8
HALF = SLOT // 2
HALO = 32
MESH = pl.DeviceIdType.MESH
COUNT, EDGE, SOUTHWARD, NORTHWARD, STATE, FORCE = range(6)


def lane_of(x):
    return lax.broadcasted_iota(jnp.int32, x.shape, 1)


def sub_of(x):
    return lax.broadcasted_iota(jnp.int32, x.shape, 0)


def lanes(x, shift):
    return pltpu.roll(x, shift % LANES, 1) if shift % LANES else x


def up(x):
    return pltpu.roll(x, x.shape[0] - 1, 0)


def down(x):
    return pltpu.roll(x, 1, 0)


def merge(parts, lane):
    bit = SLOT
    while len(parts) > 1:
        odd = lane // bit % 2 == 1
        pairs = [(parts[i], parts[i + 1]) for i in range(0, len(parts), 2)]
        parts = [b if a is None else a if b is None else jnp.where(odd, b, a) for a, b in pairs]
        bit *= 2
    return parts[0]


def kernel(
    nlon, nlat, tiles, centre,
    thick_hbm, ve_hbm, vn_hbm, cnt_hbm, height_hbm, te_hbm, tn_hbm,
    oe, on, small,
    thick, ve, vn, cnt, loads,
    rows_e, rows_n, edges, from_east, from_west, corner_in, strip, faces, keep, weights, counts,
    count_north, count_south,
    state, side_out, side_in, force, force_out, force_in, seam, plan,
    send, recv, knock,
):
    layers, r, _ = ve.shape
    groups = layers // 8
    lon, lat = lax.axis_index("lon"), lax.axis_index("lat")
    offsets = [o for o in range(centre - tiles + 1, centre + 1) if o != 0]
    own = pl.ds(centre * r, r)

    def device(dx, dy):
        return {"lon": lax.rem(lon + nlon + dx, nlon), "lat": lax.rem(lat + nlat + dy, nlat)}

    partners = [(0, o) for o in offsets] + [(-1, o) for o in [0] + offsets]
    barrier = pltpu.get_barrier_semaphore()
    for dx, dy in partners:
        pl.semaphore_signal(barrier, inc=1, device_id=device(dx, dy), device_id_type=MESH)

    @pl.when(lon < nlon - 1)
    def _():
        for o in [0] + offsets:
            pl.semaphore_signal(barrier, inc=1, device_id=device(1, o), device_id_type=MESH)

    fetched = []
    for i, far, near in (
        (0, ve_hbm, ve), (1, vn_hbm, vn), (2, cnt_hbm, cnt), (3, thick_hbm, thick),
        (4, height_hbm, state.at[1, own]), (4, te_hbm, state.at[2, own]), (4, tn_hbm, state.at[3, own]),
    ):
        fetched.append(pltpu.make_async_copy(far, near, loads.at[i]))
        fetched[-1].start()

    blank = plan.reshape(plan.shape[0] * plan.shape[1] * plan.shape[2], LANES)
    arriving = [0] * recv.shape[0]

    def sender(kind):
        return {SOUTHWARD: 1, NORTHWARD: 2}.get(kind, 0)

    def push(kind, src, dst, dx, dy, again=False):
        pltpu.make_async_remote_copy(
            src_ref=src, dst_ref=dst, send_sem=send.at[sender(kind)], recv_sem=recv.at[kind],
            device_id=device(dx, dy), device_id_type=MESH).start()
        arriving[kind] += 0 if again else math.prod(dst.shape) // LANES

    def settle(rows, sem):
        part = blank.at[pl.ds(0, rows)]
        pltpu.make_async_copy(part, part, sem).wait()

    def arrived(kind):
        settle(arriving[kind], recv.at[kind])

    low8, high8 = pl.ds(0, 8), pl.ds(r - 8, 8)
    @pl.when(lon > 0)
    def _():
        pl.semaphore_wait(barrier, len(partners) + tiles)

    @pl.when(lon == 0)
    def _():
        pl.semaphore_wait(barrier, len(partners))

    @pl.when(lon == nlon - 1)
    def _():
        for o in [0] + offsets:
            pl.semaphore_signal(knock, inc=1, device_id=device(1, o), device_id_type=MESH)

    @pl.when(lat > 0)
    def _():
        for v, buf in ((ve_hbm, rows_e), (vn_hbm, rows_n)):
            push(SOUTHWARD, v.at[:, pl.ds(0, 2)], buf.at[:, pl.ds(0, 2)], 0, -1)

    @pl.when(lat < nlat - 1)
    def _():
        for v, buf in ((ve_hbm, rows_e), (vn_hbm, rows_n)):
            push(NORTHWARD, v.at[:, pl.ds(r - 2, 2)], buf.at[:, pl.ds(6, 2)], 0, 1)

    push(COUNT, cnt_hbm.at[low8], count_north, 0, -1)
    push(COUNT, cnt_hbm.at[high8], count_south, 0, 1)

    for c in fetched[:4]:
        c.wait()

    vrows = [v.reshape(layers * r, LANES) for v in (ve, vn)]
    frows = [v.reshape(layers * 8, LANES) for v in (rows_e, rows_n)]
    orows = [v.reshape(layers * r, LANES) for v in (oe, on)]
    lane = lax.broadcasted_iota(jnp.int32, (8, LANES), 1)
    sub = lax.broadcasted_iota(jnp.int32, (8, LANES), 0)
    slot = lane // SLOT
    start = lane % SLOT < HALF

    cnt_own = cnt[...]
    counts[8:8 + r] = cnt_own.astype(jnp.float32)

    def spread_row(j):
        return jnp.broadcast_to(counts[8 + j:9 + j], (8, LANES))

    def gathered(j, column):
        parts = [None] * (LANES // SLOT)
        for f in range(2):
            for g in range(groups):
                parts[LANES // SLOT // 2 * f + g] = column(f, g)
        parts[groups] = spread_row(j)
        parts = [None if x is None else lanes(x, SLOT * i + HALF) for i, x in enumerate(parts)]
        return merge(parts, lane)

    def own_column(j):
        return lambda f, g: vrows[f][pl.ds(8 * g * r + j, 8, stride=r)]

    for j in range(r):
        strip[2 + j] = gathered(j, own_column(j))
    for i in range(r // 2):
        a, b = strip[2 + 2 * i], strip[3 + 2 * i]
        edges[0, i] = jnp.where(start, lanes(b, -HALF), a)
        edges[1, i] = jnp.where(start, a, lanes(b, HALF))
    push(EDGE, edges.at[1], from_west, 1, 0)
    for dy, at, i in ((-1, 2, 0), (1, 3, r // 2 - 1)):
        push(EDGE, edges.at[1, i], corner_in.at[at], 1, dy)

    def edges_west(again):
        push(EDGE, edges.at[0], from_east, -1, 0, again)
        for dy, at, i in ((-1, 0, 0), (1, 1, r // 2 - 1)):
            push(EDGE, edges.at[0, i], corner_in.at[at], -1, dy, again)

    @pl.when(lon > 0)
    def _():
        edges_west(False)

    zero = jnp.zeros((r, LANES), jnp.float32)

    def deepen(k, d):
        return jnp.where(k < cnt_own, d + thick[k], d)

    depth = lax.fori_loop(0, layers, deepen, zero, unroll=8)
    state[0, own] = depth
    pltpu.make_async_copy(state.at[pl.ds(1, 3), own], state.at[pl.ds(1, 3), own], loads.at[4]).wait()
    four = [depth] + [state[f, own] for f in range(1, 4)]
    slot16 = lane_of(depth)
    west_side, east_side = four[0], lanes(four[0], HALO)
    for f in range(1, 4):
        here = slot16 // HALO == f
        west_side = jnp.where(here, lanes(four[f], HALO * f), west_side)
        east_side = jnp.where(here, lanes(four[f], HALO * f + HALO), east_side)
    side_out[0] = west_side
    side_out[1] = east_side

    def rows(o):
        return pl.ds((centre - o) * r, r)

    for o in [0] + offsets:
        push(STATE, side_out.at[1], side_in.at[1, rows(o)], 1, o)

    def state_west(again):
        for o in [0] + offsets:
            push(STATE, side_out.at[0], side_in.at[0, rows(o)], -1, o, again)

    @pl.when(lon > 0)
    def _():
        state_west(False)

    for o in offsets:
        push(STATE, state.at[:, own], state.at[:, rows(o)], 0, o)

    def columns(k, carry):
        a, b = carry
        return a + thick[k] * ve[k], b + thick[k] * vn[k]

    column_e, column_n = lax.fori_loop(0, layers, columns, (zero, zero), unroll=8)
    for g in range(groups):
        w = jnp.zeros((8, LANES), jnp.float32)
        for i in range(8):
            w = jnp.where(sub == i, thick[8 * g + i], w)
        weights[g] = w

    def face_rows(low, high):
        here = [spread_row(j) for j in range(low, high + 2)]
        for i, j in enumerate(range(low, high + 1)):
            c = here[i]
            faces[0, 1 + j] = jnp.minimum(c, lanes(c, -1))
            faces[1, 1 + j] = jnp.minimum(c, here[i + 1])

    face_rows(0, r - 2)
    level_of = sub.astype(jnp.float32)

    def cross(x, n, s):
        return (lanes(x, -1) + lanes(x, 1)) + (n + s) - 4.0 * x

    def tendency(f, g, j, x, low, mid, high, wet):
        l2 = cross(mid, high, low)
        tend = jnp.where(wet, -VISCOSITY * l2, 0.0)
        orows[f][pl.ds(8 * r * g + j, 8, stride=r)] = x + tend
        return weights[g] * tend

    def wetness(f, g, j):
        return level_of + 8.0 * g.astype(jnp.float32) < faces[f, 1 + j]

    totals = [[None] * r, [None] * r]
    none = jnp.zeros((8, LANES), jnp.float32)
    for f in range(2):

        def inside(g, carry, f=f):
            x = [vrows[f][pl.ds(8 * r * g + j, 8, stride=r)] for j in range(r)]
            wet = {j: wetness(f, g, j) for j in range(1, r - 1)}
            l1 = {}
            for j in range(1, r - 1):
                l1[j] = jnp.where(wet[j], cross(x[j], x[j + 1], x[j - 1]), 0.0)
            for i, j in enumerate((1, 2, r - 3, r - 2)):
                keep[f, g, i] = l1[j]
            return tuple(
                carry[j - 2] + tendency(f, g, j, x[j], l1[j - 1], l1[j], l1[j + 1], wet[j]) for j in range(2, r - 2))

        totals[f][2:r - 2] = lax.fori_loop(0, groups, inside, (none,) * (r - 4), unroll=INNER)

    arrived(COUNT)

    @pl.when(lat > 0)
    def _():
        arrived(NORTHWARD)

    @pl.when(lat < nlat - 1)
    def _():
        arrived(SOUTHWARD)

    counts[0:8] = count_south[...].astype(jnp.float32)
    counts[8 + r:16 + r] = count_north[...].astype(jnp.float32)
    face_rows(-1, -1)
    face_rows(r - 1, r)
    for f in range(2):

        def border(g, carry, f=f):
            x = {j: vrows[f][pl.ds(8 * r * g + j, 8, stride=r)] for j in (0, 1, r - 2, r - 1)}
            for j, at in ((-2, 6), (-1, 7), (r, 0), (r + 1, 1)):
                x[j] = frows[f][pl.ds(64 * g + at, 8, stride=8)]
            wet = {j: wetness(f, g, j) for j in (-1, 0, 1, r - 2, r - 1, r)}
            l1 = {j: keep[f, g, i] for i, j in enumerate((1, 2, r - 3, r - 2))}
            for j in (-1, 0, r - 1, r):
                l1[j] = jnp.where(wet[j], cross(x[j], x[j + 1], x[j - 1]), 0.0)
            return tuple(
                carry[i] + tendency(f, g, j, x[j], l1[j - 1], l1[j], l1[j + 1], wet[j])
                for i, j in enumerate((0, 1, r - 2, r - 1)))

        found = lax.fori_loop(0, groups, border, (none,) * 4, unroll=INNER)
        for i, j in enumerate((0, 1, r - 2, r - 1)):
            totals[f][j] = found[i]
    sub16 = sub_of(zero)
    def stacked(rows_of):
        acc = zero
        for j in range(r):
            acc = jnp.where(sub16 == j, jnp.sum(rows_of[j], 0, keepdims=True), acc)
        return acc

    sum_e, sum_n = stacked(totals[0]), stacked(totals[1])
    half, middle = r // 2, LANES // 2
    scale = TIMESTEP / NSUB
    x, y = scale * sum_e, scale * sum_n
    west_side = jnp.where(slot16 < HALO, x, lanes(y, HALO))
    east_side = jnp.where(slot16 < HALO, lanes(x, HALO), lanes(y, 2 * HALO))
    front = slot16[:half] < middle
    force_out[0] = jnp.where(front, west_side[:half], lanes(west_side[half:], middle))
    force_out[1] = jnp.where(front, east_side[:half], lanes(east_side[half:], middle))
    def part(o):
        return pl.ds((centre - o) * half, half)

    for o in [0] + offsets:
        push(FORCE, force_out.at[1], force_in.at[1, part(o)], 1, o)

    def force_west(again):
        for o in [0] + offsets:
            push(FORCE, force_out.at[0], force_in.at[0, part(o)], -1, o, again)

    @pl.when(lon > 0)
    def _():
        force_west(False)

    force[0, own] = x
    force[1, own] = y
    for o in offsets:
        push(FORCE, force.at[:, own], force.at[:, rows(o)], 0, o)

    def far_column(at):
        return lambda f, g: frows[f][pl.ds(64 * g + at, 8, stride=8)]

    for j, at in ((-2, 6), (-1, 7), (r, 0), (r + 1, 1)):
        strip[2 + j] = gathered(j, far_column(at))
    @pl.when(lon == 0)
    def _():
        pl.semaphore_wait(knock, tiles)
        edges_west(True)
        state_west(True)
        force_west(True)

    arrived(EDGE)


    def unpacked(x, side, odd):
        return lanes(x, -HALF if side else HALF) if odd else x

    level_at = (SLOT * (slot % (LANES // SLOT // 2)) + sub).astype(jnp.float32)
    weight = jnp.zeros((8, LANES), jnp.float32)
    for g in range(groups):
        weight = jnp.where(slot % (LANES // SLOT // 2) == g, weights[g], weight)
    drops = []
    for side in range(2):
        source = from_west if side else from_east
        cells = []
        for j in range(-2, r + 2):
            if j < 0:
                far = unpacked(corner_in[2 * side + 1], side, j == -1)
            elif j >= r:
                far = unpacked(corner_in[2 * side], side, j == r + 1)
            else:
                far = unpacked(source[j // 2], side, j % 2)
            cells.append(jnp.where(start, far, strip[2 + j]) if side else jnp.where(start, strip[2 + j], far))
        wet, l1 = [], []
        for j in range(-1, r + 1):
            c = cells[2 + j]
            fe, fn = jnp.minimum(c, lanes(c, -1)), jnp.minimum(c, cells[3 + j])
            f = jnp.where(slot == 0, lanes(fe, -SLOT * groups), jnp.where(slot == SLOT, lanes(fn, SLOT * (SLOT - groups)), 0.0))
            for step in (SLOT, 2 * SLOT, 4 * SLOT):
                f = f + lanes(f, step)
            if side == 0 and 0 <= j < r:
                own_face = jnp.where(lane == LANES - 1, lanes(f, LANES - HALF), faces[0, 1 + j])
                small[5, j:j + 1] = own_face[:1]
                small[6, j:j + 1] = faces[1, 1 + j, 0:1]
            wet.append(level_at < f)
            l1.append(jnp.where(wet[-1], cross(c, cells[3 + j], cells[1 + j]), 0.0))
        drops.append([
            jnp.where(wet[1 + j], -VISCOSITY * cross(l1[1 + j], l1[2 + j], l1[j]), 0.0) for j in range(r)])
    found = []
    for side in range(2):
        x = stacked([weight * d for d in drops[side]])
        for step in (SLOT, 2 * SLOT, 4 * SLOT):
            x = x + lanes(x, -step)
        found.append(x)
    rim16 = (slot16 < 2) | (slot16 >= LANES - 2)
    at_start = slot16 < 2
    sum_e = jnp.where(rim16, jnp.where(at_start, lanes(found[1], -HALF), lanes(found[0], -HALF)), sum_e)
    sum_n = jnp.where(rim16, jnp.where(at_start, lanes(found[1], -HALF - middle), lanes(found[0], -HALF - middle)), sum_n)
    ends = scale * jnp.where(slot16 % middle < SLOT, found[1], lanes(found[0], SLOT))
    mine = pl.ds(centre * half, half)
    seam[mine] = jnp.where(slot16[:half] % middle < 2 * SLOT, ends[:half], lanes(ends[half:], 2 * SLOT))
    for o in offsets:
        push(FORCE, seam.at[mine], seam.at[part(o)], 0, o)
    rim = (lane < 2) | (lane >= LANES - 2)
    for j in range(r):
        ends = jnp.where(start, drops[0][j], drops[1][j])
        for f in range(2):
            for g in range(groups):
                at = pl.ds(8 * r * g + j, 8, stride=r)
                orows[f][at] = jnp.where(
                    rim, vrows[f][at] + lanes(ends, -SLOT * (SLOT * f + g) - HALF), orows[f][at])
    force_tail(tiles, centre, r, arrived, scale * sum_e, scale * sum_n, column_e + sum_e, column_n + sum_n,
               state, side_in, force, force_in, seam, plan, small)
    settle(sum(arriving) - arriving[SOUTHWARD] - arriving[NORTHWARD], send.at[0])

    @pl.when(lat > 0)
    def _():
        settle(arriving[SOUTHWARD], send.at[1])

    @pl.when(lat < nlat - 1)
    def _():
        settle(arriving[NORTHWARD], send.at[2])


INNER = 5


def force_tail(tiles, centre, r, arrived, sum_e, sum_n, column_e, column_n, state, side_in, force, force_in, seam, plan, small):
    span = tiles * r
    nv = span // 8
    own = pl.ds(centre * r, r)
    half = r // 2
    middle = LANES // 2
    lane = lane_of(sum_e)
    arrived(STATE)

    wide = lax.broadcasted_iota(jnp.int32, (span, LANES), 1)
    at_west, at_east = wide < HALO, wide >= LANES - HALO

    def blocks(mine, east, west, f):
        a = jnp.where(at_west, lanes(west, -HALO * f), lanes(mine, HALO))
        b = jnp.where(at_east, lanes(east, -HALO - HALO * f), lanes(mine, -HALO))
        return a, b

    def gate(depth, flux):
        return jnp.where(depth > 0, TIMESTEP * flux, 0.0)

    def divergence(x, y):
        return (x - lanes(x, 1)) + (y - down(y))

    def apply(m, x):
        mc, ae, aw, an, as_ = m
        return mc * x + (ae * lanes(x, -1) + aw * lanes(x, 1)) + (an * up(x) + as_ * down(x))

    square = TIMESTEP * TIMESTEP
    east, west = side_in[0], side_in[1]
    fields = [blocks(state[f], east, west, f) for f in range(4)]
    maps, ones, guess = [], [], []
    for b in range(2):
        d, h, te, tn = [x[b] for x in fields]
        de, dn = jnp.minimum(d, lanes(d, -1)), jnp.minimum(d, up(d))
        ae, an = square * de, square * dn
        aw, as_ = lanes(ae, 1), down(an)
        mc = 2.0 - ((ae + aw) + (an + as_))
        maps.append((mc, ae, aw, an, as_))
        h1 = h - divergence(gate(de, te), gate(dn, tn))
        ones.append(h1)
        guess.append(apply(maps[b], h1) - h)
        for i, x in enumerate((
            mc * mc + ((ae * ae + aw * aw) + (an * an + as_ * as_)) - 2.0,
            ae * (mc + lanes(mc, -1)), aw * (mc + lanes(mc, 1)), an * (mc + up(mc)), as_ * (mc + down(mc)),
            ae * lanes(ae, -1), aw * lanes(aw, 1), an * up(an), as_ * down(as_),
            ae * lanes(an, -1) + an * up(ae), ae * lanes(as_, -1) + as_ * down(ae),
            aw * lanes(an, 1) + an * up(aw), aw * lanes(as_, 1) + as_ * down(aw),
            h,
        )):
            plan[b, i] = x
    depth_own = state[0, own]
    over = state[0, pl.ds(((centre + 1) % tiles) * r, 8)]
    sub = sub_of(depth_own)
    depth_n = jnp.minimum(depth_own, jnp.where(
        sub == r - 1, pltpu.roll(jnp.concatenate([over] * (r // 8), 0), r - 1, 0), up(depth_own)))
    depth_e = jnp.minimum(depth_own, jnp.where(lane == LANES - 1, lanes(side_in[0, own], -1), lanes(depth_own, -1)))
    start_e, start_n = gate(depth_e, state[2, own]), gate(depth_n, state[3, own])

    arrived(FORCE)

    def unfold(x, turn):
        cuts = [x[t * half:t * half + half] for t in range(tiles)]
        return jnp.concatenate([y for c in cuts for y in (c, lanes(c, turn))], 0)

    east, west, ends = unfold(force_in[0], middle), unfold(force_in[1], middle), unfold(seam[...], -2 * SLOT)
    rim_a = (wide >= HALO - 2) & (wide < HALO + 2)
    rim_b = (wide >= LANES - HALO - 2) & (wide < LANES - HALO + 2)
    sides = []
    for f in range(2):
        a, b = blocks(force[f], east, west, f)
        a = jnp.where(rim_a, lanes(ends, HALO - HALF - middle * f), a)
        b = jnp.where(rim_b, lanes(ends, LANES - HALO - HALF - SLOT - middle * f), b)
        sides.append((a, b))
    fe, fn = sides
    drift = [divergence(fe[b], fn[b]) for b in range(2)]
    for b in range(2):
        plan[b, 14] = guess[b] - drift[b]
        plan[b, 15] = apply(maps[b], drift[b]) + 2.0 * drift[b]

    def dealt(b, i):
        return jnp.concatenate([plan[b, i, pl.ds(v, 8, stride=nv)] for v in range(nv)], 0)

    def next_row(x):
        return jnp.concatenate([x[8:], pltpu.roll(x[:8], 7, 0)], 0)

    def prior_row(x):
        return jnp.concatenate([pltpu.roll(x[span - 8:], 1, 0), x[:span - 8]], 0)

    pairs = NSUB // 2
    odd = [0] * (pairs + 1)
    for k in reversed(range(pairs)):
        odd[k] = NSUB - 2 * k - odd[k + 1]
    fixed = [[dealt(b, i) for i in range(13)] for b in range(2)]
    push_by = [dealt(b, 15) for b in range(2)]
    before = [dealt(b, 13) for b in range(2)]
    now = [dealt(b, 14) for b in range(2)]
    all_sum = [(NSUB - 1.0) * x for x in now]
    odd_sum = [float(odd[1]) * x for x in now]
    for k in range(2, pairs + 1):
        for b in range(2):
            h = now[b]
            c, e, w, n, s, ee, ww, nn, ss, en, es, wn, ws = fixed[b]
            he, hw, hn, hs = lanes(h, -1), lanes(h, 1), next_row(h), prior_row(h)
            core = (c * h - (before[b] + push_by[b])) + ((n * hn + s * hs) + (nn * next_row(hn) + ss * prior_row(hs)))
            side = (e * he + (en * next_row(he) + es * prior_row(he))) + (w * hw + (wn * next_row(hw) + ws * prior_row(hw)))
            before[b], now[b] = h, core + (side + (ee * lanes(h, -2) + ww * lanes(h, 2)))
            if k < pairs:
                odd_sum[b] += float(odd[k]) * now[b]
            all_sum[b] += (NSUB + 1.0 - 2 * k) * now[b]
    for b in range(2):
        for i, x in ((0, now[b]), (1, all_sum[b]), (2, odd_sum[b])):
            for v in range(nv):
                plan[b, i, pl.ds(v, 8, stride=nv)] = x[8 * v:8 * v + 8]

    left = lane < middle
    at = 8 if tiles >= 3 else centre * r
    low, size = (centre * r - 8, r + 16) if tiles >= 3 else (0, span)
    ends, here, easts, norths = [], [], [], []
    for b in range(2):
        m = [x[low:low + size] for x in maps[b]]
        total = (plan[b, 1, pl.ds(low, size)] + (odd[0] * ones[b][low:low + size] - float(sum(odd[1:])) * drift[b][low:low + size])
                 + apply(m, plan[b, 2, pl.ds(low, size)]))
        ends.append(plan[b, 0, own])
        here.append(total[at:at + r])
        easts.append(lanes(total, -1)[at:at + r])
        norths.append(up(total)[at:at + r])

    def joined(x):
        return jnp.where(left, lanes(x[0], -HALO), lanes(x[1], HALO))

    u, u_east, u_north = joined(here), joined(easts), joined(norths)
    ramp = NSUB * (NSUB + 1) / 2
    total_e = NSUB * start_e - square * depth_e * (u_east - u) + ramp * sum_e
    total_n = NSUB * start_n - square * depth_n * (u_north - u) + ramp * sum_n
    mean_e = total_e / (NSUB * TIMESTEP)
    mean_n = total_n / (NSUB * TIMESTEP)
    one = jnp.ones((r, LANES), jnp.float32)
    small[0] = joined(ends)
    small[1] = mean_e
    small[2] = mean_n
    small[3] = (mean_e - column_e) / (depth_e + jnp.where(depth_e > 0, 0.0, one))
    small[4] = (mean_n - column_n) / (depth_n + jnp.where(depth_n > 0, 0.0, one))


PIECES = 4


def finish(after_e, after_n, small, oe, on, oh, ome, omn, staged, sem):
    layers = after_e.shape[0]
    for i, far in enumerate((oh, ome, omn)):
        staged[2 * layers + i] = small[i]
        pltpu.make_async_copy(staged.at[2 * layers + i], far, sem).start()
    face_e, face_n = small[5], small[6]
    shift_e, shift_n = small[3], small[4]
    cuts = [layers * i // PIECES for i in range(PIECES + 1)]
    for low, high in zip(cuts, cuts[1:]):
        for k in range(low, high):
            staged[k] = jnp.where(face_e > k, after_e[k] + shift_e, 0.0)
            staged[layers + k] = jnp.where(face_n > k, after_n[k] + shift_n, 0.0)
        part = pl.ds(low, high - low)
        pltpu.make_async_copy(staged.at[part], oe.at[part], sem).start()
        pltpu.make_async_copy(staged.at[pl.ds(layers + low, high - low)], on.at[part], sem).start()
    pltpu.make_async_copy(staged, staged, sem).wait()


def solution(mesh):
    nlon, nlat = mesh.shape["lon"], mesh.shape["lat"]

    def shards(ve, vn, cnt, height, te, tn, thick):
        layers, r, width = ve.shape
        reach = -(-NSUB // r)
        tiles = min(nlat, 2 * reach + 1)
        centre = tiles // 2
        span = tiles * r
        groups = layers // 8
        f32, i32 = jnp.float32, jnp.int32
        tile = (r, width)
        vm = pltpu.VMEM
        vspec = pl.BlockSpec(memory_space=pltpu.VMEM)
        after_e, after_n, small = pl.pallas_call(
            functools.partial(kernel, nlon, nlat, tiles, centre),
            out_shape=(
                jax.ShapeDtypeStruct(ve.shape, f32),
                jax.ShapeDtypeStruct(ve.shape, f32),
                jax.ShapeDtypeStruct((7, *tile), f32),
            ),
            in_specs=[pl.BlockSpec(memory_space=pltpu.HBM)] * 7,
            out_specs=[vspec] * 3,
            scratch_shapes=[
                pltpu.SMEM((layers,), f32),
                vm(ve.shape, f32),
                vm(ve.shape, f32),
                vm(tile, i32),
                pltpu.SemaphoreType.DMA((5,)),
                vm((layers, 8, width), f32),
                vm((layers, 8, width), f32),
                vm((2, r // 2, 8, width), f32),
                vm((r // 2, 8, width), f32),
                vm((r // 2, 8, width), f32),
                vm((4, 8, width), f32),
                vm((r + 4, 8, width), f32),
                vm((2, r + 2, 8, width), f32),
                vm((2, groups, 4, 8, width), f32),
                vm((groups, 8, width), f32),
                vm((r + 16, width), f32),
                vm((8, width), i32),
                vm((8, width), i32),
                vm((4, span, width), f32),
                vm((2, *tile), f32),
                vm((2, span, width), f32),
                vm((2, span, width), f32),
                vm((2, r // 2, width), f32),
                vm((2, span // 2, width), f32),
                vm((span // 2, width), f32),
                vm((2, 17, span, width), f32),
                pltpu.SemaphoreType.DMA((3,)),
                pltpu.SemaphoreType.DMA((6,)),
                pltpu.SemaphoreType.REGULAR,
            ],
            compiler_params=pltpu.CompilerParams(
                collective_id=0, has_side_effects=True, vmem_limit_bytes=16 << 20),
        )(*[pltpu.with_memory_space_constraint(x, pltpu.HBM) for x in (thick, ve, vn, cnt, height, te, tn)])
        out = jax.ShapeDtypeStruct(tile, f32)
        levels = jax.ShapeDtypeStruct(ve.shape, f32)
        return pl.pallas_call(
            finish,
            out_shape=(levels, levels, out, out, out),
            in_specs=[vspec] * 3,
            out_specs=[pl.BlockSpec(memory_space=pltpu.HBM)] * 5,
            scratch_shapes=[vm((2 * layers + 3, *tile), f32), pltpu.SemaphoreType.DMA],
            compiler_params=pltpu.CompilerParams(vmem_limit_bytes=16 << 20),
        )(after_e, after_n, small)

    level = P(None, "lat", "lon")
    flat = P("lat", "lon")
    return jax.shard_map(
        shards,
        mesh=mesh,
        in_specs=(level, level, flat, flat, flat, flat, P()),
        out_specs=(level, level, flat, flat, flat),
        check_vma=False,
    )
```

```python
import functools
import math

import jax
import jax.numpy as jnp
from jax import lax
from jax.experimental import pallas as pl
from jax.experimental.pallas import tpu as pltpu
from jax.sharding import PartitionSpec as P

NSUB = 30
VISCOSITY = 0.01
TIMESTEP = 0.35
LANES = 128
SLOT = 8
HALF = SLOT // 2
HALO = 32
MESH = pl.DeviceIdType.MESH
COUNT, EDGE, SOUTHWARD, NORTHWARD, STATE, FORCE = range(6)


def lane_of(x):
    return lax.broadcasted_iota(jnp.int32, x.shape, 1)


def sub_of(x):
    return lax.broadcasted_iota(jnp.int32, x.shape, 0)


def lanes(x, shift):
    return pltpu.roll(x, shift % LANES, 1) if shift % LANES else x


def up(x):
    return pltpu.roll(x, x.shape[0] - 1, 0)


def down(x):
    return pltpu.roll(x, 1, 0)


def merge(parts, lane):
    bit = SLOT
    while len(parts) > 1:
        odd = lane // bit % 2 == 1
        pairs = [(parts[i], parts[i + 1]) for i in range(0, len(parts), 2)]
        parts = [b if a is None else a if b is None else jnp.where(odd, b, a) for a, b in pairs]
        bit *= 2
    return parts[0]


def kernel(
    nlon, nlat, tiles, centre,
    thick_hbm, ve_hbm, vn_hbm, cnt_hbm, height_hbm, te_hbm, tn_hbm,
    oe, on, small,
    thick, ve, vn, cnt, loads,
    rows_e, rows_n, edges, from_east, from_west, corner_in, strip, faces, keep, weights, counts,
    count_north, count_south,
    state, side_out, side_in, force, force_out, force_in, seam, plan,
    send, recv, knock,
):
    layers, r, _ = ve.shape
    groups = layers // 8
    lon, lat = lax.axis_index("lon"), lax.axis_index("lat")
    offsets = [o for o in range(centre - tiles + 1, centre + 1) if o != 0]
    own = pl.ds(centre * r, r)

    def device(dx, dy):
        return {"lon": lax.rem(lon + nlon + dx, nlon), "lat": lax.rem(lat + nlat + dy, nlat)}

    partners = [(0, o) for o in offsets] + [(-1, o) for o in [0] + offsets]
    barrier = pltpu.get_barrier_semaphore()
    for dx, dy in partners:
        pl.semaphore_signal(barrier, inc=1, device_id=device(dx, dy), device_id_type=MESH)

    @pl.when(lon < nlon - 1)
    def _():
        for o in [0] + offsets:
            pl.semaphore_signal(barrier, inc=1, device_id=device(1, o), device_id_type=MESH)

    fetched = []
    for i, far, near in (
        (0, ve_hbm, ve), (1, vn_hbm, vn), (2, cnt_hbm, cnt), (3, thick_hbm, thick),
        (4, height_hbm, state.at[1, own]), (4, te_hbm, state.at[2, own]), (4, tn_hbm, state.at[3, own]),
    ):
        fetched.append(pltpu.make_async_copy(far, near, loads.at[i]))
        fetched[-1].start()

    blank = plan.reshape(plan.shape[0] * plan.shape[1] * plan.shape[2], LANES)
    arriving = [0] * recv.shape[0]

    def sender(kind):
        return {SOUTHWARD: 1, NORTHWARD: 2}.get(kind, 0)

    def push(kind, src, dst, dx, dy, again=False):
        pltpu.make_async_remote_copy(
            src_ref=src, dst_ref=dst, send_sem=send.at[sender(kind)], recv_sem=recv.at[kind],
            device_id=device(dx, dy), device_id_type=MESH).start()
        arriving[kind] += 0 if again else math.prod(dst.shape) // LANES

    def settle(rows, sem):
        part = blank.at[pl.ds(0, rows)]
        pltpu.make_async_copy(part, part, sem).wait()

    def arrived(kind):
        settle(arriving[kind], recv.at[kind])

    low8, high8 = pl.ds(0, 8), pl.ds(r - 8, 8)
    @pl.when(lon > 0)
    def _():
        pl.semaphore_wait(barrier, len(partners) + tiles)

    @pl.when(lon == 0)
    def _():
        pl.semaphore_wait(barrier, len(partners))

    @pl.when(lon == nlon - 1)
    def _():
        for o in [0] + offsets:
            pl.semaphore_signal(knock, inc=1, device_id=device(1, o), device_id_type=MESH)

    @pl.when(lat > 0)
    def _():
        for v, buf in ((ve_hbm, rows_e), (vn_hbm, rows_n)):
            push(SOUTHWARD, v.at[:, pl.ds(0, 2)], buf.at[:, pl.ds(0, 2)], 0, -1)

    @pl.when(lat < nlat - 1)
    def _():
        for v, buf in ((ve_hbm, rows_e), (vn_hbm, rows_n)):
            push(NORTHWARD, v.at[:, pl.ds(r - 2, 2)], buf.at[:, pl.ds(6, 2)], 0, 1)

    push(COUNT, cnt_hbm.at[low8], count_north, 0, -1)
    push(COUNT, cnt_hbm.at[high8], count_south, 0, 1)

    for c in fetched[:4]:
        c.wait()

    vrows = [v.reshape(layers * r, LANES) for v in (ve, vn)]
    frows = [v.reshape(layers * 8, LANES) for v in (rows_e, rows_n)]
    orows = [v.reshape(layers * r, LANES) for v in (oe, on)]
    lane = lax.broadcasted_iota(jnp.int32, (8, LANES), 1)
    sub = lax.broadcasted_iota(jnp.int32, (8, LANES), 0)
    slot = lane // SLOT
    start = lane % SLOT < HALF

    cnt_own = cnt[...]
    counts[8:8 + r] = cnt_own.astype(jnp.float32)

    def spread_row(j):
        return jnp.broadcast_to(counts[8 + j:9 + j], (8, LANES))

    def gathered(j, column):
        parts = [None] * (LANES // SLOT)
        for f in range(2):
            for g in range(groups):
                parts[LANES // SLOT // 2 * f + g] = column(f, g)
        parts[groups] = spread_row(j)
        parts = [None if x is None else lanes(x, SLOT * i + HALF) for i, x in enumerate(parts)]
        return merge(parts, lane)

    def own_column(j):
        return lambda f, g: vrows[f][pl.ds(8 * g * r + j, 8, stride=r)]

    for j in range(r):
        strip[2 + j] = gathered(j, own_column(j))
    for i in range(r // 2):
        a, b = strip[2 + 2 * i], strip[3 + 2 * i]
        edges[0, i] = jnp.where(start, lanes(b, -HALF), a)
        edges[1, i] = jnp.where(start, a, lanes(b, HALF))
    push(EDGE, edges.at[1], from_west, 1, 0)
    for dy, at, i in ((-1, 2, 0), (1, 3, r // 2 - 1)):
        push(EDGE, edges.at[1, i], corner_in.at[at], 1, dy)

    def edges_west(again):
        push(EDGE, edges.at[0], from_east, -1, 0, again)
        for dy, at, i in ((-1, 0, 0), (1, 1, r // 2 - 1)):
            push(EDGE, edges.at[0, i], corner_in.at[at], -1, dy, again)

    @pl.when(lon > 0)
    def _():
        edges_west(False)

    zero = jnp.zeros((r, LANES), jnp.float32)

    def deepen(k, d):
        return jnp.where(k < cnt_own, d + thick[k], d)

    depth = lax.fori_loop(0, layers, deepen, zero, unroll=8)
    state[0, own] = depth
    pltpu.make_async_copy(state.at[pl.ds(1, 3), own], state.at[pl.ds(1, 3), own], loads.at[4]).wait()
    four = [depth] + [state[f, own] for f in range(1, 4)]
    slot16 = lane_of(depth)
    west_side, east_side = four[0], lanes(four[0], HALO)
    for f in range(1, 4):
        here = slot16 // HALO == f
        west_side = jnp.where(here, lanes(four[f], HALO * f), west_side)
        east_side = jnp.where(here, lanes(four[f], HALO * f + HALO), east_side)
    side_out[0] = west_side
    side_out[1] = east_side

    def rows(o):
        return pl.ds((centre - o) * r, r)

    for o in [0] + offsets:
        push(STATE, side_out.at[1], side_in.at[1, rows(o)], 1, o)

    def state_west(again):
        for o in [0] + offsets:
            push(STATE, side_out.at[0], side_in.at[0, rows(o)], -1, o, again)

    @pl.when(lon > 0)
    def _():
        state_west(False)

    for o in offsets:
        push(STATE, state.at[:, own], state.at[:, rows(o)], 0, o)

    def columns(k, carry):
        a, b = carry
        return a + thick[k] * ve[k], b + thick[k] * vn[k]

    column_e, column_n = lax.fori_loop(0, layers, columns, (zero, zero), unroll=8)
    for g in range(groups):
        w = jnp.zeros((8, LANES), jnp.float32)
        for i in range(8):
            w = jnp.where(sub == i, thick[8 * g + i], w)
        weights[g] = w

    def face_rows(low, high):
        here = [spread_row(j) for j in range(low, high + 2)]
        for i, j in enumerate(range(low, high + 1)):
            c = here[i]
            faces[0, 1 + j] = jnp.minimum(c, lanes(c, -1))
            faces[1, 1 + j] = jnp.minimum(c, here[i + 1])

    face_rows(0, r - 2)
    level_of = sub.astype(jnp.float32)

    def cross(x, n, s):
        return (lanes(x, -1) + lanes(x, 1)) + (n + s) - 4.0 * x

    def tendency(f, g, j, x, low, mid, high, wet):
        l2 = cross(mid, high, low)
        tend = jnp.where(wet, -VISCOSITY * l2, 0.0)
        orows[f][pl.ds(8 * r * g + j, 8, stride=r)] = x + tend
        return weights[g] * tend

    def wetness(f, g, j):
        return level_of + 8.0 * g.astype(jnp.float32) < faces[f, 1 + j]

    totals = [[None] * r, [None] * r]
    none = jnp.zeros((8, LANES), jnp.float32)
    for f in range(2):

        def inside(g, carry, f=f):
            x = [vrows[f][pl.ds(8 * r * g + j, 8, stride=r)] for j in range(r)]
            wet = {j: wetness(f, g, j) for j in range(1, r - 1)}
            l1 = {}
            for j in range(1, r - 1):
                l1[j] = jnp.where(wet[j], cross(x[j], x[j + 1], x[j - 1]), 0.0)
            for i, j in enumerate((1, 2, r - 3, r - 2)):
                keep[f, g, i] = l1[j]
            return tuple(
                carry[j - 2] + tendency(f, g, j, x[j], l1[j - 1], l1[j], l1[j + 1], wet[j]) for j in range(2, r - 2))

        totals[f][2:r - 2] = lax.fori_loop(0, groups, inside, (none,) * (r - 4), unroll=INNER)

    arrived(COUNT)

    @pl.when(lat > 0)
    def _():
        arrived(NORTHWARD)

    @pl.when(lat < nlat - 1)
    def _():
        arrived(SOUTHWARD)

    counts[0:8] = count_south[...].astype(jnp.float32)
    counts[8 + r:16 + r] = count_north[...].astype(jnp.float32)
    face_rows(-1, -1)
    face_rows(r - 1, r)
    for f in range(2):

        def border(g, carry, f=f):
            x = {j: vrows[f][pl.ds(8 * r * g + j, 8, stride=r)] for j in (0, 1, r - 2, r - 1)}
            for j, at in ((-2, 6), (-1, 7), (r, 0), (r + 1, 1)):
                x[j] = frows[f][pl.ds(64 * g + at, 8, stride=8)]
            wet = {j: wetness(f, g, j) for j in (-1, 0, 1, r - 2, r - 1, r)}
            l1 = {j: keep[f, g, i] for i, j in enumerate((1, 2, r - 3, r - 2))}
            for j in (-1, 0, r - 1, r):
                l1[j] = jnp.where(wet[j], cross(x[j], x[j + 1], x[j - 1]), 0.0)
            return tuple(
                carry[i] + tendency(f, g, j, x[j], l1[j - 1], l1[j], l1[j + 1], wet[j])
                for i, j in enumerate((0, 1, r - 2, r - 1)))

        found = lax.fori_loop(0, groups, border, (none,) * 4, unroll=INNER)
        for i, j in enumerate((0, 1, r - 2, r - 1)):
            totals[f][j] = found[i]
    sub16 = sub_of(zero)
    def stacked(rows_of):
        acc = zero
        for j in range(r):
            acc = jnp.where(sub16 == j, jnp.sum(rows_of[j], 0, keepdims=True), acc)
        return acc

    sum_e, sum_n = stacked(totals[0]), stacked(totals[1])
    half, middle = r // 2, LANES // 2
    scale = TIMESTEP / NSUB
    x, y = scale * sum_e, scale * sum_n
    west_side = jnp.where(slot16 < HALO, x, lanes(y, HALO))
    east_side = jnp.where(slot16 < HALO, lanes(x, HALO), lanes(y, 2 * HALO))
    front = slot16[:half] < middle
    force_out[0] = jnp.where(front, west_side[:half], lanes(west_side[half:], middle))
    force_out[1] = jnp.where(front, east_side[:half], lanes(east_side[half:], middle))
    def part(o):
        return pl.ds((centre - o) * half, half)

    for o in [0] + offsets:
        push(FORCE, force_out.at[1], force_in.at[1, part(o)], 1, o)

    def force_west(again):
        for o in [0] + offsets:
            push(FORCE, force_out.at[0], force_in.at[0, part(o)], -1, o, again)

    @pl.when(lon > 0)
    def _():
        force_west(False)

    force[0, own] = x
    force[1, own] = y
    for o in offsets:
        push(FORCE, force.at[:, own], force.at[:, rows(o)], 0, o)

    def far_column(at):
        return lambda f, g: frows[f][pl.ds(64 * g + at, 8, stride=8)]

    for j, at in ((-2, 6), (-1, 7), (r, 0), (r + 1, 1)):
        strip[2 + j] = gathered(j, far_column(at))
    @pl.when(lon == 0)
    def _():
        pl.semaphore_wait(knock, tiles)
        edges_west(True)
        state_west(True)
        force_west(True)

    arrived(EDGE)


    def unpacked(x, side, odd):
        return lanes(x, -HALF if side else HALF) if odd else x

    level_at = (SLOT * (slot % (LANES // SLOT // 2)) + sub).astype(jnp.float32)
    weight = jnp.zeros((8, LANES), jnp.float32)
    for g in range(groups):
        weight = jnp.where(slot % (LANES // SLOT // 2) == g, weights[g], weight)
    drops = []
    for side in range(2):
        source = from_west if side else from_east
        cells = []
        for j in range(-2, r + 2):
            if j < 0:
                far = unpacked(corner_in[2 * side + 1], side, j == -1)
            elif j >= r:
                far = unpacked(corner_in[2 * side], side, j == r + 1)
            else:
                far = unpacked(source[j // 2], side, j % 2)
            cells.append(jnp.where(start, far, strip[2 + j]) if side else jnp.where(start, strip[2 + j], far))
        wet, l1 = [], []
        for j in range(-1, r + 1):
            c = cells[2 + j]
            fe, fn = jnp.minimum(c, lanes(c, -1)), jnp.minimum(c, cells[3 + j])
            f = jnp.where(slot == 0, lanes(fe, -SLOT * groups), jnp.where(slot == SLOT, lanes(fn, SLOT * (SLOT - groups)), 0.0))
            for step in (SLOT, 2 * SLOT, 4 * SLOT):
                f = f + lanes(f, step)
            if side == 0 and 0 <= j < r:
                own_face = jnp.where(lane == LANES - 1, lanes(f, LANES - HALF), faces[0, 1 + j])
                small[5, j:j + 1] = own_face[:1]
                small[6, j:j + 1] = faces[1, 1 + j, 0:1]
            wet.append(level_at < f)
            l1.append(jnp.where(wet[-1], cross(c, cells[3 + j], cells[1 + j]), 0.0))
        drops.append([
            jnp.where(wet[1 + j], -VISCOSITY * cross(l1[1 + j], l1[2 + j], l1[j]), 0.0) for j in range(r)])
    found = []
    for side in range(2):
        x = stacked([weight * d for d in drops[side]])
        for step in (SLOT, 2 * SLOT, 4 * SLOT):
            x = x + lanes(x, -step)
        found.append(x)
    rim16 = (slot16 < 2) | (slot16 >= LANES - 2)
    at_start = slot16 < 2
    sum_e = jnp.where(rim16, jnp.where(at_start, lanes(found[1], -HALF), lanes(found[0], -HALF)), sum_e)
    sum_n = jnp.where(rim16, jnp.where(at_start, lanes(found[1], -HALF - middle), lanes(found[0], -HALF - middle)), sum_n)
    ends = scale * jnp.where(slot16 % middle < SLOT, found[1], lanes(found[0], SLOT))
    mine = pl.ds(centre * half, half)
    seam[mine] = jnp.where(slot16[:half] % middle < 2 * SLOT, ends[:half], lanes(ends[half:], 2 * SLOT))
    for o in offsets:
        push(FORCE, seam.at[mine], seam.at[part(o)], 0, o)
    def patch():
        rim = (lane < 2) | (lane >= LANES - 2)
        for j in range(r):
            ends = jnp.where(start, drops[0][j], drops[1][j])
            for f in range(2):
                for g in range(groups):
                    at = pl.ds(8 * r * g + j, 8, stride=r)
                    orows[f][at] = jnp.where(
                        rim, vrows[f][at] + lanes(ends, -SLOT * (SLOT * f + g) - HALF), orows[f][at])

    force_tail(tiles, centre, r, arrived, scale * sum_e, scale * sum_n, column_e + sum_e, column_n + sum_n,
               state, side_in, force, force_in, seam, plan, small, patch)
    settle(sum(arriving) - arriving[SOUTHWARD] - arriving[NORTHWARD], send.at[0])

    @pl.when(lat > 0)
    def _():
        settle(arriving[SOUTHWARD], send.at[1])

    @pl.when(lat < nlat - 1)
    def _():
        settle(arriving[NORTHWARD], send.at[2])


INNER = 5


def force_tail(tiles, centre, r, arrived, sum_e, sum_n, column_e, column_n, state, side_in, force, force_in, seam, plan, small, patch):
    span = tiles * r
    nv = span // 8
    own = pl.ds(centre * r, r)
    half = r // 2
    middle = LANES // 2
    lane = lane_of(sum_e)
    arrived(STATE)

    wide = lax.broadcasted_iota(jnp.int32, (span, LANES), 1)
    at_west, at_east = wide < HALO, wide >= LANES - HALO

    def blocks(mine, east, west, f):
        a = jnp.where(at_west, lanes(west, -HALO * f), lanes(mine, HALO))
        b = jnp.where(at_east, lanes(east, -HALO - HALO * f), lanes(mine, -HALO))
        return a, b

    def gate(depth, flux):
        return jnp.where(depth > 0, TIMESTEP * flux, 0.0)

    def divergence(x, y):
        return (x - lanes(x, 1)) + (y - down(y))

    def apply(m, x):
        mc, ae, aw, an, as_ = m
        return mc * x + (ae * lanes(x, -1) + aw * lanes(x, 1)) + (an * up(x) + as_ * down(x))

    square = TIMESTEP * TIMESTEP
    east, west = side_in[0], side_in[1]
    fields = [blocks(state[f], east, west, f) for f in range(4)]
    maps, ones, guess = [], [], []
    for b in range(2):
        d, h, te, tn = [x[b] for x in fields]
        de, dn = jnp.minimum(d, lanes(d, -1)), jnp.minimum(d, up(d))
        ae, an = square * de, square * dn
        aw, as_ = lanes(ae, 1), down(an)
        mc = 2.0 - ((ae + aw) + (an + as_))
        maps.append((mc, ae, aw, an, as_))
        h1 = h - divergence(gate(de, te), gate(dn, tn))
        ones.append(h1)
        guess.append(apply(maps[b], h1) - h)
        for i, x in enumerate((
            mc * mc + ((ae * ae + aw * aw) + (an * an + as_ * as_)) - 2.0,
            ae * (mc + lanes(mc, -1)), aw * (mc + lanes(mc, 1)), an * (mc + up(mc)), as_ * (mc + down(mc)),
            ae * lanes(ae, -1), aw * lanes(aw, 1), an * up(an), as_ * down(as_),
            ae * lanes(an, -1) + an * up(ae), ae * lanes(as_, -1) + as_ * down(ae),
            aw * lanes(an, 1) + an * up(aw), aw * lanes(as_, 1) + as_ * down(aw),
            h,
        )):
            plan[b, i] = x
    depth_own = state[0, own]
    over = state[0, pl.ds(((centre + 1) % tiles) * r, 8)]
    sub = sub_of(depth_own)
    depth_n = jnp.minimum(depth_own, jnp.where(
        sub == r - 1, pltpu.roll(jnp.concatenate([over] * (r // 8), 0), r - 1, 0), up(depth_own)))
    depth_e = jnp.minimum(depth_own, jnp.where(lane == LANES - 1, lanes(side_in[0, own], -1), lanes(depth_own, -1)))
    start_e, start_n = gate(depth_e, state[2, own]), gate(depth_n, state[3, own])

    patch()
    arrived(FORCE)

    def unfold(x, turn):
        cuts = [x[t * half:t * half + half] for t in range(tiles)]
        return jnp.concatenate([y for c in cuts for y in (c, lanes(c, turn))], 0)

    east, west, ends = unfold(force_in[0], middle), unfold(force_in[1], middle), unfold(seam[...], -2 * SLOT)
    rim_a = (wide >= HALO - 2) & (wide < HALO + 2)
    rim_b = (wide >= LANES - HALO - 2) & (wide < LANES - HALO + 2)
    sides = []
    for f in range(2):
        a, b = blocks(force[f], east, west, f)
        a = jnp.where(rim_a, lanes(ends, HALO - HALF - middle * f), a)
        b = jnp.where(rim_b, lanes(ends, LANES - HALO - HALF - SLOT - middle * f), b)
        sides.append((a, b))
    fe, fn = sides
    drift = [divergence(fe[b], fn[b]) for b in range(2)]
    for b in range(2):
        plan[b, 14] = guess[b] - drift[b]
        plan[b, 15] = apply(maps[b], drift[b]) + 2.0 * drift[b]

    def dealt(b, i):
        return jnp.concatenate([plan[b, i, pl.ds(v, 8, stride=nv)] for v in range(nv)], 0)

    def next_row(x):
        return jnp.concatenate([x[8:], pltpu.roll(x[:8], 7, 0)], 0)

    def prior_row(x):
        return jnp.concatenate([pltpu.roll(x[span - 8:], 1, 0), x[:span - 8]], 0)

    pairs = NSUB // 2
    odd = [0] * (pairs + 1)
    for k in reversed(range(pairs)):
        odd[k] = NSUB - 2 * k - odd[k + 1]
    fixed = [[dealt(b, i) for i in range(13)] for b in range(2)]
    push_by = [dealt(b, 15) for b in range(2)]
    before = [dealt(b, 13) for b in range(2)]
    now = [dealt(b, 14) for b in range(2)]
    all_sum = [(NSUB - 1.0) * x for x in now]
    odd_sum = [float(odd[1]) * x for x in now]
    for k in range(2, pairs + 1):
        for b in range(2):
            h = now[b]
            c, e, w, n, s, ee, ww, nn, ss, en, es, wn, ws = fixed[b]
            he, hw, hn, hs = lanes(h, -1), lanes(h, 1), next_row(h), prior_row(h)
            core = (c * h - (before[b] + push_by[b])) + ((n * hn + s * hs) + (nn * next_row(hn) + ss * prior_row(hs)))
            side = (e * he + (en * next_row(he) + es * prior_row(he))) + (w * hw + (wn * next_row(hw) + ws * prior_row(hw)))
            before[b], now[b] = h, core + (side + (ee * lanes(h, -2) + ww * lanes(h, 2)))
            if k < pairs:
                odd_sum[b] += float(odd[k]) * now[b]
            all_sum[b] += (NSUB + 1.0 - 2 * k) * now[b]
    for b in range(2):
        for i, x in ((0, now[b]), (1, all_sum[b]), (2, odd_sum[b])):
            for v in range(nv):
                plan[b, i, pl.ds(v, 8, stride=nv)] = x[8 * v:8 * v + 8]

    left = lane < middle
    at = 8 if tiles >= 3 else centre * r
    low, size = (centre * r - 8, r + 16) if tiles >= 3 else (0, span)
    ends, here, easts, norths = [], [], [], []
    for b in range(2):
        m = [x[low:low + size] for x in maps[b]]
        total = (plan[b, 1, pl.ds(low, size)] + (odd[0] * ones[b][low:low + size] - float(sum(odd[1:])) * drift[b][low:low + size])
                 + apply(m, plan[b, 2, pl.ds(low, size)]))
        ends.append(plan[b, 0, own])
        here.append(total[at:at + r])
        easts.append(lanes(total, -1)[at:at + r])
        norths.append(up(total)[at:at + r])

    def joined(x):
        return jnp.where(left, lanes(x[0], -HALO), lanes(x[1], HALO))

    u, u_east, u_north = joined(here), joined(easts), joined(norths)
    ramp = NSUB * (NSUB + 1) / 2
    total_e = NSUB * start_e - square * depth_e * (u_east - u) + ramp * sum_e
    total_n = NSUB * start_n - square * depth_n * (u_north - u) + ramp * sum_n
    mean_e = total_e / (NSUB * TIMESTEP)
    mean_n = total_n / (NSUB * TIMESTEP)
    one = jnp.ones((r, LANES), jnp.float32)
    small[0] = joined(ends)
    small[1] = mean_e
    small[2] = mean_n
    small[3] = (mean_e - column_e) / (depth_e + jnp.where(depth_e > 0, 0.0, one))
    small[4] = (mean_n - column_n) / (depth_n + jnp.where(depth_n > 0, 0.0, one))


PIECES = 4


def finish(after_e, after_n, small, oe, on, oh, ome, omn, staged, sem):
    layers = after_e.shape[0]
    for i, far in enumerate((oh, ome, omn)):
        staged[2 * layers + i] = small[i]
        pltpu.make_async_copy(staged.at[2 * layers + i], far, sem).start()
    face_e, face_n = small[5], small[6]
    shift_e, shift_n = small[3], small[4]
    cuts = [layers * i // PIECES for i in range(PIECES + 1)]
    for low, high in zip(cuts, cuts[1:]):
        for k in range(low, high):
            staged[k] = jnp.where(face_e > k, after_e[k] + shift_e, 0.0)
            staged[layers + k] = jnp.where(face_n > k, after_n[k] + shift_n, 0.0)
        part = pl.ds(low, high - low)
        pltpu.make_async_copy(staged.at[part], oe.at[part], sem).start()
        pltpu.make_async_copy(staged.at[pl.ds(layers + low, high - low)], on.at[part], sem).start()
    pltpu.make_async_copy(staged, staged, sem).wait()


def solution(mesh):
    nlon, nlat = mesh.shape["lon"], mesh.shape["lat"]

    def shards(ve, vn, cnt, height, te, tn, thick):
        layers, r, width = ve.shape
        reach = -(-NSUB // r)
        tiles = min(nlat, 2 * reach + 1)
        centre = tiles // 2
        span = tiles * r
        groups = layers // 8
        f32, i32 = jnp.float32, jnp.int32
        tile = (r, width)
        vm = pltpu.VMEM
        vspec = pl.BlockSpec(memory_space=pltpu.VMEM)
        after_e, after_n, small = pl.pallas_call(
            functools.partial(kernel, nlon, nlat, tiles, centre),
            out_shape=(
                jax.ShapeDtypeStruct(ve.shape, f32),
                jax.ShapeDtypeStruct(ve.shape, f32),
                jax.ShapeDtypeStruct((7, *tile), f32),
            ),
            in_specs=[pl.BlockSpec(memory_space=pltpu.HBM)] * 7,
            out_specs=[vspec] * 3,
            scratch_shapes=[
                pltpu.SMEM((layers,), f32),
                vm(ve.shape, f32),
                vm(ve.shape, f32),
                vm(tile, i32),
                pltpu.SemaphoreType.DMA((5,)),
                vm((layers, 8, width), f32),
                vm((layers, 8, width), f32),
                vm((2, r // 2, 8, width), f32),
                vm((r // 2, 8, width), f32),
                vm((r // 2, 8, width), f32),
                vm((4, 8, width), f32),
                vm((r + 4, 8, width), f32),
                vm((2, r + 2, 8, width), f32),
                vm((2, groups, 4, 8, width), f32),
                vm((groups, 8, width), f32),
                vm((r + 16, width), f32),
                vm((8, width), i32),
                vm((8, width), i32),
                vm((4, span, width), f32),
                vm((2, *tile), f32),
                vm((2, span, width), f32),
                vm((2, span, width), f32),
                vm((2, r // 2, width), f32),
                vm((2, span // 2, width), f32),
                vm((span // 2, width), f32),
                vm((2, 17, span, width), f32),
                pltpu.SemaphoreType.DMA((3,)),
                pltpu.SemaphoreType.DMA((6,)),
                pltpu.SemaphoreType.REGULAR,
            ],
            compiler_params=pltpu.CompilerParams(
                collective_id=0, has_side_effects=True, vmem_limit_bytes=16 << 20),
        )(*[pltpu.with_memory_space_constraint(x, pltpu.HBM) for x in (thick, ve, vn, cnt, height, te, tn)])
        out = jax.ShapeDtypeStruct(tile, f32)
        levels = jax.ShapeDtypeStruct(ve.shape, f32)
        return pl.pallas_call(
            finish,
            out_shape=(levels, levels, out, out, out),
            in_specs=[vspec] * 3,
            out_specs=[pl.BlockSpec(memory_space=pltpu.HBM)] * 5,
            scratch_shapes=[vm((2 * layers + 3, *tile), f32), pltpu.SemaphoreType.DMA],
            compiler_params=pltpu.CompilerParams(vmem_limit_bytes=16 << 20),
        )(after_e, after_n, small)

    level = P(None, "lat", "lon")
    flat = P("lat", "lon")
    return jax.shard_map(
        shards,
        mesh=mesh,
        in_specs=(level, level, flat, flat, flat, flat, P()),
        out_specs=(level, level, flat, flat, flat),
        check_vma=False,
    )
```
